512 devices in a mesh: img: 16 (over z, core), ori: 32 (over x, y).
Axes of the slice: x: 4, y: 8, z: 8, core: 2. Of those that a mesh axis runs over, the one named last changes fastest.
Arguments:
- images: bfloat16 [1024, 16384], P(('img', 'ori')), may hold values from -8 to 8
- references: bfloat16 [512, 16384], P('ori'), may hold values from -6 to 6
- shifts: float32 [12, 2], replicated, may hold values from -3 to 3
- owners: int32 [65536, 1], P(('ori', 'img')), may hold values from 0 to 31; in each aligned block of 128 rows (0 to 127, 128 to 255, ...) at most 16 rows name the same one
- slot_rows: int32 [65536], P(('ori', 'img')), may hold values from 0 to 63
- interpolation: float32 [65536, 128], P(('ori', 'img')), may hold values from -0.5 to 0.5
- regularizer: float32 [32768], P(('ori', 'img')), may hold values from 1 to 16
Outputs:
- volume: float32 [32768, 128], P(('ori', 'img'))
- resampled: float32 [512, 16384], P(('ori', 'img'))
The draws below stay inside these ranges and needn't reach their ends.
Inputs may be any that keep to these rules, and one draw needn't show every extreme that they name: `owners`: among the 128 segments of one device (aligned blocks of rows), no owner is named more than 16 times, a bound that some block reaches.
All inputs are finite; a program needn't handle non-finite values.
Results may differ from the reference program's by a relative error of at most 0.014.
Values may be sent and summed in bfloat16 or wider, within the bound.
A program may use at most 64 MiB of HBM per device.

```python
import math
import jax
import jax.numpy as jnp
import numpy as np
from jax import lax

COEF = 16384
SEGLEN = 128
SHIFTS = 12
O_DEV = 16
IMG_DEV = 2
SEGS = 128
ORIENT = 512
IMAGES = 1024
SEG_DEV = 128
CAP = 16
VR_DEV = 64
VROWS = 32768
NSEG = 65536
N_IMG = 16
N_ORI = 32
DEVICES = 512


grid_width = 64


image_side = 128.0


def phase_tables_drawn(shifts):
    half_len = COEF // 2
    positions = jnp.arange(half_len, dtype=jnp.int32)
    freq_x = (positions % grid_width).astype(jnp.float32)
    freq_y = (positions // grid_width - half_len // grid_width // 2).astype(jnp.float32)
    angles = 2.0 * math.pi / image_side * (shifts[:, 0:1] * freq_x[None, :] + shifts[:, 1:2] * freq_y[None, :])
    return (jnp.cos(angles), jnp.sin(angles))


def common_references(key):
    ref_key = jax.random.fold_in(key, 11)
    values = jnp.clip(jax.random.normal(ref_key, (ORIENT, COEF), jnp.float32), -6.0, 6.0)
    return values


def common_shifts(key):
    return jax.random.uniform(jax.random.fold_in(key, 12), (SHIFTS, 2), jnp.float32, -3.0, 3.0)


def draw_references(key, part):
    return common_references(key).astype(jnp.bfloat16)


def draw_shifts(key, part):
    return common_shifts(key)


def aligned_rows(key, base):
    refs_rounded = common_references(key).astype(jnp.bfloat16).astype(jnp.float32)
    cosine_table, sine_table = phase_tables_drawn(common_shifts(key))
    keys_list = jax.random.split(jax.random.fold_in(key, 14), 5)
    first_pick = jax.random.randint(keys_list[0], (IMAGES,), 0, ORIENT)
    second_pick = (first_pick + 1 + jax.random.randint(keys_list[1], (IMAGES,), 0, ORIENT - 1)) % ORIENT
    shift_pick = jax.random.randint(keys_list[2], (IMAGES,), 0, SHIFTS)
    chosen = jax.random.randint(keys_list[3], (IMAGES,), 0, 16) == 0
    amplify = math.sqrt(16384.0 / COEF)
    strength = amplify * jax.random.uniform(keys_list[4], (IMAGES,), jnp.float32, 0.6, 1.5)
    half_len = COEF // 2
    paired = refs_rounded[first_pick] + refs_rounded[second_pick]
    cos_rows = cosine_table[shift_pick]
    sin_rows = sine_table[shift_pick]
    aligned_re = paired[:, :half_len] * cos_rows - paired[:, half_len:] * sin_rows
    aligned_im = paired[:, :half_len] * sin_rows + paired[:, half_len:] * cos_rows
    aligned = jnp.clip(strength[:, None] * jnp.concatenate([aligned_re, aligned_im], axis=1), -8.0, 8.0)
    return jnp.where(chosen[:, None], aligned, base)


def draw_images(key, part):
    image_key = jax.random.fold_in(key, 13)
    base = jnp.clip(jax.random.normal(image_key, (IMAGES, COEF), jnp.float32), -6.0, 6.0)
    values = aligned_rows(key, base)
    return values.astype(jnp.bfloat16)


def plant(drawn, key, least, largest):
    extent = drawn.shape
    spot = [jax.random.randint(jax.random.fold_in(key, axis), (), 0, extent[axis]) for axis in range(len(extent))]
    drawn = drawn.at[tuple(spot)].set(least)
    longest = extent.index(max(extent))
    spot[longest] = (spot[longest] + 1) % extent[longest]
    return drawn.at[tuple(spot)].set(largest)


def steps_of(stream_key, extent, cuts, least, high):
    level, own = 1.0, jax.random.fold_in(stream_key, 6)
    for dim, blocks in cuts:
        steps = jnp.exp(jax.random.uniform(jax.random.fold_in(own, dim), (blocks,), jnp.float32, least / len(cuts), high / len(cuts)))
        level = level * jnp.repeat(steps, extent[dim] // blocks).reshape([-1 if axis == dim else 1 for axis in range(len(extent))])
    return level


def routed_block(key, own, number, rows, number_of, top, most, skew):
    sequence = jax.random.permutation(key, number_of)
    packed, common = load_shares(number_of, rows * top, most, skew, True), load_shares(number_of, rows * top, most, skew, False)
    places = jnp.arange(number_of)

    def named(tallies, offset_by):
        used = int((tallies > 0).sum())
        fixed = max(1, used // 4)
        shifted = fixed + (places - fixed + offset_by * (used - fixed)) % max(1, number_of - fixed)
        return jnp.zeros((number_of,), jnp.int32).at[sequence[jnp.where(places < fixed, places, shifted)]].set(jnp.asarray(tallies, jnp.int32))

    tallies = jnp.where(number % 4 == 0, named(packed, number // 4), named(common, number - number // 4 - 1))
    mixed = jax.random.permutation(jax.random.fold_in(own, 3), number_of)
    giver, receiver = mixed[0:number_of // 2 * 2:2], mixed[1:number_of // 2 * 2:2]
    room = jnp.minimum(tallies[giver] - 1, most - tallies[receiver]) // 2
    room = jnp.where((giver == sequence[0]) | (receiver == sequence[0]) | (tallies[receiver] == 0), 0, jnp.maximum(room, 0))
    shifted = jax.random.randint(jax.random.fold_in(own, 4), (number_of // 2,), 0, 1 << 20) % (room + 1)
    tallies = tallies.at[giver].add(-shifted).at[receiver].add(shifted)
    members = jnp.searchsorted(jnp.cumsum(tallies), jnp.arange(rows * top), side="right").astype(jnp.int32)
    table = members.reshape(top, rows).T
    table = table[jax.random.permutation(jax.random.fold_in(own, 1), rows)]
    offset_by = jax.random.randint(jax.random.fold_in(own, 2), (rows, 1), 0, top)
    return jnp.take_along_axis(table, (jnp.arange(top)[None, :] + offset_by) % top, axis=1)


def load_shares(number_of, total, bound, skew, full):
    weights = [(1 << 20) // math.isqrt(standing ** skew) + 1 for standing in range(1, number_of + 1)]
    largest = bound if full else min(bound, max(-(-total // number_of), total * weights[0] // sum(weights)))
    least = 1 if total - largest >= number_of - 1 else 0
    holding, spare = [largest] + [least] * (number_of - 1), total - largest - least * (number_of - 1)
    while spare > 0:
        movable = [i for i in range(1, number_of) if holding[i] < largest] or [i for i in range(1, number_of) if holding[i] < bound]
        mass, left = sum([weights[i] for i in movable]), spare
        for i in movable:
            more = min(bound - holding[i], max(1, left * weights[i] // mass), spare)
            holding[i] = holding[i] + more
            spare = spare - more
    return np.array(holding)


def centred(rng, dims, scale, most, shards=(), kind=jnp.bfloat16):
    drawn = jax.random.normal(rng, dims, jnp.float32) * scale
    if len(shards) > 0:
        drawn = steps_of(rng, dims, shards, -0.22, 0.18) * drawn
    return jnp.clip(drawn, min=-most, max=most).astype(kind)


def setup_inputs(seed: int = 0) -> dict:
    key_list = jax.random.split(jax.random.key(seed), 8)
    images = draw_images(jax.random.fold_in(key_list[7], 71), 0)
    references = draw_references(jax.random.fold_in(key_list[7], 71), 0)
    shifts = draw_shifts(jax.random.fold_in(key_list[7], 71), 0)
    owners_keys = jax.random.split(jax.random.fold_in(key_list[3], 1), NSEG // SEG_DEV)
    owners_turns = jax.random.permutation(jax.random.fold_in(key_list[3], 3), NSEG // SEG_DEV)
    owners = jax.vmap(lambda own, number: routed_block(jax.random.fold_in(key_list[3], 2), own, number, SEG_DEV, N_ORI, 1, CAP, 2))(owners_keys, owners_turns).reshape((NSEG, 1))
    slot_rows = plant(jax.random.randint(key_list[4], (NSEG,), 0, VR_DEV), jax.random.fold_in(key_list[4], 1), 0, VR_DEV - 1).astype(jnp.int32)
    interpolation = centred(key_list[5], (DEVICES * SEGLEN, SEGLEN), SEGLEN ** -0.5, 0.5, ((0, 512),), jnp.float32)
    regularizer = jnp.clip(jnp.exp(math.log(16.0) - 2.7725887 * jax.random.uniform(key_list[6], (VROWS,), jnp.float32) ** steps_of(key_list[6], (VROWS,), ((0, 512),), -0.2, 0.2)), 1.0, 16.0)
    return dict(images=images, references=references, shifts=shifts, owners=owners, slot_rows=slot_rows, interpolation=interpolation, regularizer=regularizer)


grid_width = 64
image_side = 128.0

def phase_tables(shifts):
    half_len = COEF // 2
    positions = jnp.arange(half_len, dtype=jnp.int32)
    freq_x = (positions % grid_width).astype(jnp.float32)
    freq_y = (positions // grid_width - half_len // grid_width // 2).astype(jnp.float32)
    angles = 2.0 * math.pi / image_side * (shifts[:, 0:1] * freq_x[None, :] + shifts[:, 1:2] * freq_y[None, :])
    return (jnp.cos(angles), jnp.sin(angles))

def shifted_slices(references, cosine_table, sine_table):
    half_len = COEF // 2
    real_part = references[:, :half_len].astype(jnp.float32)
    imag_part = references[:, half_len:].astype(jnp.float32)
    rotated_re = real_part[:, None, :] * cosine_table[None] - imag_part[:, None, :] * sine_table[None]
    rotated_im = real_part[:, None, :] * sine_table[None] + imag_part[:, None, :] * cosine_table[None]
    stacked = jnp.concatenate([rotated_re, rotated_im], axis=2)
    return stacked.reshape(-1, COEF).astype(jnp.bfloat16)

def backproject(weights_b, group_images, cosine_table, sine_table):
    half_len = COEF // 2
    orient_count = weights_b.shape[1]
    total_re = jnp.zeros((orient_count, half_len), jnp.float32)
    total_im = jnp.zeros((orient_count, half_len), jnp.float32)
    for shift_number in range(SHIFTS):
        summed = lax.dot_general(weights_b[:, :, shift_number], group_images, (((0,), (0,)), ((), ())), preferred_element_type=jnp.float32)
        sum_re = summed[:, :half_len]
        sum_im = summed[:, half_len:]
        total_re = total_re + sum_re * cosine_table[shift_number] + sum_im * sine_table[shift_number]
        total_im = total_im - sum_re * sine_table[shift_number] + sum_im * cosine_table[shift_number]
    return jnp.concatenate([total_re, total_im], axis=1)

def reference(images, references, shifts, owners, slot_rows, interpolation, regularizer):
    cosine_table, sine_table = phase_tables(shifts)
    rotated = shifted_slices(references, cosine_table, sine_table)
    score_scale = 2.0 / math.sqrt(COEF)
    group_rows = IMG_DEV * N_ORI
    grouped = images.reshape(N_IMG, group_rows, COEF)

    def one_group(running, group_images):
        scores = lax.dot_general(group_images, rotated, (((1,), (1,)), ((), ())), preferred_element_type=jnp.float32) * score_scale
        row_peak = lax.optimization_barrier(jnp.max(scores, axis=1, keepdims=True))
        exponent = jnp.exp(scores - row_peak)
        weights = exponent / lax.optimization_barrier(jnp.sum(exponent, axis=1, keepdims=True))
        weights3 = weights.reshape(group_rows, ORIENT, SHIFTS)
        orient_mass = lax.optimization_barrier(jnp.sum(weights3, axis=(0, 2)))
        summed = backproject(weights3.astype(jnp.bfloat16), group_images, cosine_table, sine_table)
        return ((running[0] + summed, running[1] + orient_mass), None)
    start_state = (jnp.zeros((ORIENT, COEF), jnp.float32), jnp.zeros((ORIENT,), jnp.float32))
    (slices, orient_mass), _ = lax.scan(one_group, start_state, grouped)
    device_count = N_IMG * N_ORI
    total_rows = regularizer.shape[0]
    brick_rows = total_rows // device_count
    seg_device = O_DEV // N_IMG * SEGS
    segments = slices.reshape(ORIENT * SEGS, SEGLEN)
    seg_mass = jnp.repeat(orient_mass, SEGS)
    positions = jnp.arange(ORIENT * SEGS, dtype=jnp.int32)
    group_of = positions // seg_device % N_IMG
    target = ((owners[:, 0] * N_IMG + group_of) * brick_rows + slot_rows).astype(jnp.int32)
    inserted = jnp.zeros((total_rows, SEGLEN), jnp.float32).at[target].add(segments)
    weight_sum = jnp.zeros((total_rows,), jnp.float32).at[target].add(seg_mass)
    kernels = interpolation.reshape(device_count, SEGLEN, SEGLEN)
    mapped = jnp.einsum('drk,dkl->drl', inserted.reshape(device_count, brick_rows, SEGLEN), kernels, precision=lax.Precision.HIGHEST)
    volume = mapped.reshape(total_rows, SEGLEN) / (weight_sum + regularizer)[:, None]
    back_values = jnp.einsum('drl,dkl->drk', volume.reshape(device_count, brick_rows, SEGLEN), kernels, precision=lax.Precision.HIGHEST)
    resampled = back_values.reshape(total_rows, SEGLEN)[target].reshape(ORIENT, COEF)
    return (volume, resampled)
```

```python
import heapq
import math

import jax
import jax.numpy as jnp
from jax import lax
from jax.experimental import pallas as pl
from jax.experimental.pallas import tpu as pltpu
from jax.sharding import PartitionSpec as P

NX, NY, NZ = 4, 8, 8
N_ORI = NX * NY
N_IMG = 2 * NZ
COEF = 16384
QUART = COEF // 4
SHIFTS = 12
CAP = 16
SLOTS = N_ORI * CAP
ROWS = 64
MESH = pl.DeviceIdType.MESH
HIGH = lax.Precision.HIGHEST
F32, BF16 = jnp.float32, jnp.bfloat16

WIDTH = {"A+": 768, "A-": 768, "B+": 1280, "B-": 1280}
ROUTES = tuple(WIDTH)
START = {"A+": 0, "A-": 768, "B+": 1536, "B-": 2816}


def forwards(route, dx, dy):
    plus = route[1] == "+"
    up_x, down_x = ((0, 1), (0,)) if plus else ((0,), (0, 3))
    up_y, down_y = ((0, 1, 2, 3), (0, 7, 6)) if plus else ((0, 1, 2), (0, 7, 6, 5))
    out = []
    along_x = route[0] == "A" and dy == 0 or route[0] == "B"
    along_y = route[0] == "B" and dx == 0 or route[0] == "A"
    if along_y:
        if dy in up_y:
            out.append(("+y", dx, (dy + 1) % NY))
        if dy in down_y:
            out.append(("-y", dx, (dy - 1) % NY))
    if along_x:
        if dx in up_x:
            out.append(("+x", (dx + 1) % NX, dy))
        if dx in down_x:
            out.append(("-x", (dx - 1) % NX, dy))
    return out


def depth(route, dx, dy):
    return max((1 + depth(route, a, b) for _, a, b in forwards(route, dx, dy)), default=0)


def gather_plan():
    heap = [(0.0, i, r, 0, 0) for i, r in enumerate(("B+", "B-", "A+", "A-"))]
    free = dict.fromkeys(("+x", "-x", "+y", "-y"), 0.0)
    plan, count = [], 10
    while heap:
        when, _, route, dx, dy = heapq.heappop(heap)
        hops = sorted(forwards(route, dx, dy), key=lambda f: -depth(route, f[1], f[2]))
        plan.append((route, dx, dy, hops))
        for link, a, b in hops:
            free[link] = max(when, free[link]) + WIDTH[route] * 16 / 46.5e3 + 0.05
            count += 1
            heapq.heappush(heap, (free[link] + 1.6, count, route, a, b))
    return plan


def iota(shape, dim):
    return lax.broadcasted_iota(jnp.int32, shape, dim)


def kernel(
    img, refs, shifts, owners, slot_rows, interp, reg,
    vol, res,
    gat, rot, cos_t, sin_t, acc, wts, prod, part, own_tot, pair_s, pair_r, z_s, z_r,
    meta_s, meta_r, stat_s, stat_r, mz_s, mz_r, mb_s, mb_r, val_s, val_r, rep_s, rep_r,
    oh, oh_t, scat, scat_t, cnt,
    loc_sem, gat_send, gat_recv, pair_send, pair_recv, z_send, z_recv, sends, recvs,
):
    me_i, me_o = lax.axis_index("img"), lax.axis_index("ori")
    x, y = me_o // NY, lax.rem(me_o, NY)
    z, c = me_i // 2, lax.rem(me_i, 2)

    barrier = pltpu.get_barrier_semaphore()

    def greet_ori(p, carry):
        pl.semaphore_signal(barrier, 1, device_id={"ori": lax.rem(me_o + p, N_ORI)}, device_id_type=MESH)
        return carry

    def greet_img(p, carry):
        pl.semaphore_signal(barrier, 1, device_id={"img": lax.rem(me_i + p, N_IMG)}, device_id_type=MESH)
        return carry

    lax.fori_loop(1, N_ORI, greet_ori, 0)
    lax.fori_loop(1, N_IMG, greet_img, 0)

    own_copy = pltpu.make_async_copy(img, gat.at[me_o], loc_sem)
    own_copy.start()

    unit = 2.0 * math.pi / 128.0
    step_x, step_y = unit * shifts[:, 0:1], unit * shifts[:, 1:2]
    lane12 = iota((SHIFTS, 128), 1)
    base = step_x * (lane12 % 64).astype(F32) + step_y * (lane12 // 64).astype(F32)
    tile = step_y * (2 * lane12 - 64).astype(F32)
    base_c, base_s, tile_c, tile_s = jnp.cos(base), jnp.sin(base), jnp.cos(tile), jnp.sin(tile)
    for t in range(64):
        half, col = t // 32, (t % 32) * 128
        tc, ts = tile_c[:, t : t + 1], tile_s[:, t : t + 1]
        cos_t[half, :, col : col + 128] = base_c * tc - base_s * ts
        sin_t[half, :, col : col + 128] = base_s * tc + base_c * ts

    def rotate(step, carry):
        cols = pl.ds(pl.multiple_of(step * 256, 256), 256)
        for half in range(2):
            real = refs[:, pl.ds(pl.multiple_of(half * QUART + step * 256, 256), 256)].astype(F32)
            imag = refs[:, pl.ds(pl.multiple_of((2 + half) * QUART + step * 256, 256), 256)].astype(F32)
            for s in range(SHIFTS):
                cs, sn = cos_t[half, s : s + 1, cols], sin_t[half, s : s + 1, cols]
                rot[pl.ds(half * 192 + s * 16, 16), cols] = (real * cs - imag * sn).astype(BF16)
                rot[pl.ds((2 + half) * 192 + s * 16, 16), cols] = (real * sn + imag * cs).astype(BF16)
        return carry

    lax.fori_loop(0, QUART // 256, rotate, 0)

    eye = iota((128, 128), 0) == iota((128, 128), 1)
    row_col = jnp.sum(jnp.where(eye, slot_rows[...].astype(F32), 0.0), axis=1, keepdims=True)
    blocks = [(q * 32 + u * 8) for u in range(4) for q in range(4)]
    row_col = jnp.concatenate([row_col[b : b + 8] for b in blocks], axis=0)
    own_col = jnp.concatenate([owners[b : b + 8, :] for b in blocks], axis=0).astype(F32)
    lane128 = iota((128, 128), 1).astype(F32)
    owner_hot = (own_col == lane128).astype(F32)
    before = (iota((128, 128), 1) < iota((128, 128), 0)).astype(BF16)
    counts = jnp.dot(before, owner_hot.astype(BF16), preferred_element_type=F32)
    rank_col = jnp.sum(counts * owner_hot, axis=1, keepdims=True)
    slot_col = own_col * CAP + rank_col
    slot_row = jnp.sum(jnp.where(eye, slot_col, 0.0), axis=0, keepdims=True)
    oh[...] = (slot_row == iota((SLOTS, 128), 0).astype(F32)).astype(BF16)
    oh_t[...] = (slot_col == iota((128, SLOTS), 1).astype(F32)).astype(BF16)
    rank_rows = jnp.where(rank_col == lane128, row_col + 1.0, 0.0).astype(BF16)
    table = lax.dot_general(
        owner_hot.astype(BF16), rank_rows, (((0,), (0,)), ((), ())), preferred_element_type=F32
    ) - 1.0
    for d in range(N_ORI):
        meta_s[d] = table[d : d + 1, :]

    own_copy.wait()
    pl.semaphore_wait(barrier, N_ORI - 1 + N_IMG - 1)

    link = {
        "+x": lax.rem(x + 1, NX) * NY + y,
        "-x": lax.rem(x + NX - 1, NX) * NY + y,
        "+y": x * NY + lax.rem(y + 1, NY),
        "-y": x * NY + lax.rem(y + NY - 1, NY),
    }

    def gather_copy(route, dx, dy, to, there):
        src = lax.rem(x + NX - dx, NX) * NY + lax.rem(y + NY - dy, NY)
        ref = gat.at[src, :, pl.ds(START[route], WIDTH[route])]
        r = ROUTES.index(route)
        return pltpu.make_async_remote_copy(
            src_ref=ref, dst_ref=ref, send_sem=gat_send.at[r], recv_sem=gat_recv.at[r, there],
            device_id={"ori": to}, device_id_type=MESH,
        )

    def spread(send_ref, recv_ref, number):
        def one(p, carry):
            to = lax.rem(me_o + p, N_ORI)
            src = send_ref.at[0] if send_ref.shape[0] == 1 else send_ref.at[to]
            pltpu.make_async_remote_copy(
                src_ref=src, dst_ref=recv_ref.at[me_o], send_sem=sends.at[number], recv_sem=recvs.at[number],
                device_id={"ori": to}, device_id_type=MESH,
            ).start()
            return carry

        lax.fori_loop(1, N_ORI, one, 0)

    def await_bytes(ref, sem):
        pltpu.make_async_copy(ref, ref, sem).wait()

    for route, dx, dy, hops in gather_plan():
        if dx or dy:
            gather_copy(route, dx, dy, me_o, dx * NY + dy).wait_recv()
        for name, a, b in hops:
            gather_copy(route, dx, dy, link[name], a * NY + b).start()
        if (route, dx, dy) == ("A-", 0, 0):
            spread(meta_s, meta_r, 0)
            meta_r[me_o] = meta_s[me_o]

    acc[...] = jnp.zeros_like(acc)

    def score(step, carry):
        cols = pl.ds(pl.multiple_of(step * 512, 512), 512)
        block = gat[:, :, cols].reshape(N_ORI * 8, 512)
        acc[...] += lax.dot_general(rot[:, cols], block, (((1,), (1,)), ((), ())), preferred_element_type=F32)
        return carry

    lax.fori_loop(0, QUART // 512, score, 0)

    lane = iota((192, 256), 1)
    mine = jnp.zeros((192, 256), F32)
    for q in range(4):
        mine = mine + jnp.where(lane % 4 == q, acc[q * 192 : (q + 1) * 192, :], 0.0)
    fold = (iota((256, 256), 0) // 4 == iota((256, 256), 1) // 4).astype(F32)
    scores = jnp.dot(mine, fold, precision=HIGH, preferred_element_type=F32) * (2.0 / math.sqrt(COEF))
    peak = jnp.max(scores, axis=0, keepdims=True)
    expo = jnp.exp(scores - peak)
    total = jnp.sum(expo, axis=0, keepdims=True)
    stat = jnp.where(iota((1, 256), 1) % 2 == 0, peak, total)
    stat_s[0] = stat
    spread(stat_s, stat_r, 1)
    stat_r[me_o] = stat

    await_bytes(meta_r.at[pl.ds(0, N_ORI - 1)], recvs.at[0])
    rep = (iota((SLOTS, N_ORI), 0) // CAP == iota((SLOTS, N_ORI), 1)).astype(BF16)
    rid = jnp.dot(rep, meta_r[...].reshape(N_ORI, 128).astype(BF16), preferred_element_type=F32)
    rid = jnp.where(iota((SLOTS, 128), 0) % CAP == iota((SLOTS, 128), 1), rid, 0.0)
    hot = (jnp.sum(rid, axis=1, keepdims=True) == iota((SLOTS, 128), 1).astype(F32)).astype(F32)
    scat_t[...] = hot.astype(BF16)
    scat[...] = jnp.transpose(hot).astype(BF16)
    cnt[...] = jnp.dot(scat[...], rep, preferred_element_type=F32)
    reg_col = jnp.sum(
        jnp.where(iota((ROWS, ROWS), 0) == iota((ROWS, ROWS), 1), reg[...], 0.0), axis=1, keepdims=True
    )

    await_bytes(stat_r.at[pl.ds(0, N_ORI - 1)], recvs.at[1])
    stats = stat_r[...].reshape(N_ORI, 256)
    even = iota((N_ORI, 256), 1) % 2 == 0
    peaks = jnp.where(even, stats, pltpu.roll(stats, 1, 1))
    totals = jnp.where(even, pltpu.roll(stats, 255, 1), stats)
    top = jnp.max(peaks, axis=0, keepdims=True)
    whole = jnp.sum(totals * jnp.exp(peaks - top), axis=0, keepdims=True)
    weights = expo * (jnp.exp(peak - top) / whole)
    for q in range(4):
        wts[q * 192 : (q + 1) * 192, :] = jnp.where(lane % 4 == q, weights, 0.0).astype(BF16)

    mass = jnp.sum(jnp.where(lane % 4 == 0, weights, 0.0), axis=1, keepdims=True)
    mass16 = mass[0:16]
    for s in range(1, SHIFTS):
        mass16 = mass16 + mass[s * 16 : s * 16 + 16]
    mass16 = jnp.broadcast_to(mass16, (16, 128))
    for o in range(N_IMG):
        mz_s[o] = mass16[o : o + 1, :]

    def send_mass(p, carry):
        to = lax.rem(me_i + p, N_IMG)
        pltpu.make_async_remote_copy(
            src_ref=mz_s.at[to], dst_ref=mz_r.at[me_i], send_sem=sends.at[2], recv_sem=recvs.at[2],
            device_id={"img": to}, device_id_type=MESH,
        ).start()
        return carry

    lax.fori_loop(1, N_IMG, send_mass, 0)
    mz_r[me_i] = mz_s[me_i]

    def pair_copy(u):
        return pltpu.make_async_remote_copy(
            src_ref=pair_s.at[u], dst_ref=pair_r.at[u], send_sem=pair_send.at[u], recv_sem=pair_recv.at[u],
            device_id={"img": z * 2 + 1 - c}, device_id_type=MESH,
        )

    def project(u, carry):
        for v in range(4):
            cols = pl.ds(pl.multiple_of(u * 1024 + v * 256, 256), 256)
            block = gat[:, :, cols].reshape(N_ORI * 8, 256)
            prod[...] = jnp.dot(wts[...], block, preferred_element_type=F32)
            for half in range(2):
                re = jnp.zeros((16, 256), F32)
                im = jnp.zeros((16, 256), F32)
                for s in range(SHIFTS):
                    cs, sn = cos_t[half, s : s + 1, cols], sin_t[half, s : s + 1, cols]
                    sr = prod[half * 192 + s * 16 : half * 192 + s * 16 + 16, :]
                    si = prod[(2 + half) * 192 + s * 16 : (2 + half) * 192 + s * 16 + 16, :]
                    re = re + sr * cs + si * sn
                    im = im - sr * sn + si * cs
                for a in range(2):
                    part[u, :, half * 8 + v * 2 + a, :] = re[:, a * 128 : a * 128 + 128]
                    part[u, :, (2 + half) * 8 + v * 2 + a, :] = im[:, a * 128 : a * 128 + 128]
        for k in range(NZ):
            pair_s[u, k] = part[u, 2 * k + 1 - c].astype(BF16)
        pair_copy(u).start()
        return carry

    def reduce_pair(u):
        pair_copy(u).wait_recv()
        own_tot[u] = part[u, 2 * z + c] + pair_r[u, z].astype(F32)
        for p in (4, 3, 5, 2, 6, 1, 7):
            to = lax.rem(z + p, NZ)
            z_s[u, to] = (part[u, 2 * to + c] + pair_r[u, to].astype(F32)).astype(BF16)
            pltpu.make_async_remote_copy(
                src_ref=z_s.at[u, to], dst_ref=z_r.at[u, z], send_sem=z_send.at[u], recv_sem=z_recv.at[u],
                device_id={"img": to * 2 + c}, device_id_type=MESH,
            ).start()

    def project_and_reduce(u, carry):
        project(u, 0)
        reduce_pair(u - 1)
        return carry

    project(0, 0)
    lax.fori_loop(1, 4, project_and_reduce, 0)
    reduce_pair(3)

    await_bytes(mz_r.at[pl.ds(0, N_IMG - 1)], recvs.at[2])
    mass_all = jnp.sum(mz_r[...].reshape(N_IMG, 128), axis=0, keepdims=True)
    mb_s[0] = mass_all
    spread(mb_s, mb_r, 3)
    mb_r[me_o] = mass_all

    sums = []
    for u in range(4):
        await_bytes(z_r.at[u, pl.ds(0, NZ - 1)], z_recv.at[u])
        tot = own_tot[u]
        for p in range(1, NZ):
            tot = tot + z_r[u, lax.rem(z + p, NZ)].astype(F32)
        sums.append(tot)
    segments = jnp.concatenate(sums, axis=0).astype(BF16)

    val_s[...] = jnp.dot(oh[...], segments, preferred_element_type=F32).astype(BF16).reshape(N_ORI, CAP, 128)
    spread(val_s, val_r, 4)
    val_r[me_o] = val_s[me_o]

    await_bytes(mb_r.at[pl.ds(0, N_ORI - 1)], recvs.at[3])
    weight_sum = jnp.dot(
        cnt[0:ROWS, :], mb_r[...].reshape(N_ORI, 128), precision=HIGH, preferred_element_type=F32
    )
    denom = weight_sum + reg_col

    await_bytes(val_r.at[pl.ds(0, N_ORI - 1)], recvs.at[4])
    inserted = jnp.dot(scat[0:ROWS, :], val_r[...].reshape(SLOTS, 128), preferred_element_type=F32)
    mapped = jnp.dot(inserted, interp[...], precision=HIGH, preferred_element_type=F32)
    volume = mapped / denom
    vol[...] = volume
    back = lax.dot_general(
        volume, interp[...], (((1,), (1,)), ((), ())), precision=HIGH, preferred_element_type=F32
    )
    reply = jnp.dot(scat_t[:, 0:ROWS], back.astype(BF16), preferred_element_type=F32)
    rep_s[...] = reply.astype(BF16).reshape(N_ORI, CAP, 128)
    spread(rep_s, rep_r, 5)
    rep_r[me_o] = rep_s[me_o]

    for r, route in enumerate(ROUTES):
        await_bytes(gat.at[pl.ds(0, N_ORI - 1), :, pl.ds(START[route], WIDTH[route])], gat_send.at[r])
    for u in range(4):
        pair_copy(u).wait_send()
        await_bytes(z_s.at[u, pl.ds(0, NZ - 1)], z_send.at[u])
    await_bytes(meta_s.at[pl.ds(0, N_ORI - 1)], sends.at[0])
    await_bytes(stat_r.at[pl.ds(0, N_ORI - 1)], sends.at[1])
    await_bytes(mz_s.at[pl.ds(0, N_IMG - 1)], sends.at[2])
    await_bytes(mb_r.at[pl.ds(0, N_ORI - 1)], sends.at[3])
    await_bytes(val_s.at[pl.ds(0, N_ORI - 1)], sends.at[4])

    await_bytes(rep_r.at[pl.ds(0, N_ORI - 1)], recvs.at[5])
    picked = jnp.dot(oh_t[...], rep_r[...].reshape(SLOTS, 128), preferred_element_type=F32)
    for u in range(4):
        for q in range(4):
            res[q * 32 + u * 8 : q * 32 + u * 8 + 8, :] = picked[u * 32 + q * 8 : u * 32 + q * 8 + 8, :]
    await_bytes(rep_s.at[pl.ds(0, N_ORI - 1)], sends.at[5])


def shards(images, references, shifts, owners, slot_rows, interpolation, regularizer):
    vmem = pl.BlockSpec(memory_space=pltpu.VMEM)
    volume, resampled = pl.pallas_call(
        kernel,
        out_shape=(jax.ShapeDtypeStruct((ROWS, 128), F32), jax.ShapeDtypeStruct((128, 128), F32)),
        in_specs=[vmem] * 7,
        out_specs=(vmem, vmem),
        scratch_shapes=[
            pltpu.VMEM((N_ORI, 8, QUART), BF16),
            pltpu.VMEM((768, QUART), BF16),
            pltpu.VMEM((2, SHIFTS, QUART), F32),
            pltpu.VMEM((2, SHIFTS, QUART), F32),
            pltpu.VMEM((768, 256), F32),
            pltpu.VMEM((768, 256), BF16),
            pltpu.VMEM((768, 256), F32),
            pltpu.VMEM((4, N_IMG, 32, 128), F32),
            pltpu.VMEM((4, 32, 128), F32),
            pltpu.VMEM((4, NZ, 32, 128), BF16),
            pltpu.VMEM((4, NZ, 32, 128), BF16),
            pltpu.VMEM((4, NZ, 32, 128), BF16),
            pltpu.VMEM((4, NZ, 32, 128), BF16),
            pltpu.VMEM((N_ORI, 1, 128), F32),
            pltpu.VMEM((N_ORI, 1, 128), F32),
            pltpu.VMEM((1, 1, 256), F32),
            pltpu.VMEM((N_ORI, 1, 256), F32),
            pltpu.VMEM((N_IMG, 1, 128), F32),
            pltpu.VMEM((N_IMG, 1, 128), F32),
            pltpu.VMEM((1, 1, 128), F32),
            pltpu.VMEM((N_ORI, 1, 128), F32),
            pltpu.VMEM((N_ORI, CAP, 128), BF16),
            pltpu.VMEM((N_ORI, CAP, 128), BF16),
            pltpu.VMEM((N_ORI, CAP, 128), BF16),
            pltpu.VMEM((N_ORI, CAP, 128), BF16),
            pltpu.VMEM((SLOTS, 128), BF16),
            pltpu.VMEM((128, SLOTS), BF16),
            pltpu.VMEM((128, SLOTS), BF16),
            pltpu.VMEM((SLOTS, 128), BF16),
            pltpu.VMEM((128, N_ORI), F32),
            pltpu.SemaphoreType.DMA,
            pltpu.SemaphoreType.DMA((4,)),
            pltpu.SemaphoreType.DMA((4, N_ORI)),
            pltpu.SemaphoreType.DMA((4,)),
            pltpu.SemaphoreType.DMA((4,)),
            pltpu.SemaphoreType.DMA((4,)),
            pltpu.SemaphoreType.DMA((4,)),
            pltpu.SemaphoreType.DMA((6,)),
            pltpu.SemaphoreType.DMA((6,)),
        ],
        compiler_params=pltpu.CompilerParams(
            collective_id=0, has_side_effects=True, vmem_limit_bytes=48 * 1024 * 1024
        ),
    )(
        images.reshape(8, QUART),
        references,
        shifts,
        owners,
        slot_rows.reshape(1, 128),
        interpolation,
        regularizer.reshape(1, ROWS),
    )
    return (volume, resampled.reshape(1, COEF))


def solution(mesh):
    in_specs = (
        P(("img", "ori"), None),
        P("ori", None),
        P(),
        P(("ori", "img"), None),
        P(("ori", "img")),
        P(("ori", "img"), None),
        P(("ori", "img")),
    )
    out_specs = (P(("ori", "img"), None), P(("ori", "img"), None))
    return jax.shard_map(shards, mesh=mesh, in_specs=in_specs, out_specs=out_specs, check_vma=False)
```

```python
import heapq
import math

import jax
import jax.numpy as jnp
from jax import lax
from jax.experimental import pallas as pl
from jax.experimental.pallas import tpu as pltpu
from jax.sharding import PartitionSpec as P

NX, NY, NZ = 4, 8, 8
N_ORI = NX * NY
N_IMG = 2 * NZ
COEF = 16384
QUART = COEF // 4
SHIFTS = 12
CAP = 16
SLOTS = N_ORI * CAP
ROWS = 64
MESH = pl.DeviceIdType.MESH
SCORE_COLS = 2048
HIGH = lax.Precision.HIGHEST
F32, BF16 = jnp.float32, jnp.bfloat16

SPLIT = 1536
RANGE = {"A": (0, SPLIT), "B": (SPLIT, QUART)}
PARENT = {"A": ((0, 0, 1), (0, 0, 1, 2, 2)), "B": ((0, 0, 1), (0, 0, 0, 2, 2))}


def ring_steps(parents, size, d, sign, lo, hi, mid):
    for k in range(1, size // 2 + 1):
        for way in (1, -1):
            if d != way * parents[k] % size or d and sign != way:
                continue
            a, b = lo, hi
            if k == size // 2:
                a, b = (lo, min(hi, mid)) if way > 0 else (max(lo, mid), hi)
            if a < b:
                yield way, way * k % size, k - parents[k], a, b


def forwards(block):
    route, lo, hi, dx, dy, sx, sy = block
    mid = sum(RANGE[route]) // 2
    par_x, par_y = PARENT[route]
    out = []
    if route == "A" or dx == 0:
        for way, d, hops, a, b in ring_steps(par_y, NY, dy, sy, lo, hi, mid):
            out.append(("y", way * hops, (route, a, b, dx, d, sx, way)))
    if route == "B" or dy == 0:
        for way, d, hops, a, b in ring_steps(par_x, NX, dx, sx, lo, hi, mid):
            out.append(("x", way * hops, (route, a, b, d, dy, way, sy)))
    return out


def depth(block):
    return max((1.4 + 0.7 * abs(h) + depth(k) for _, h, k in forwards(block)), default=0)


def gather_plan():
    heap = [(0.0, i, (r, *RANGE[r], 0, 0, 0, 0)) for i, r in enumerate("BA")]
    free, plan, count = {}, [], 10
    while heap:
        when, _, block = heapq.heappop(heap)
        hops = sorted(forwards(block), key=lambda f: -depth(f[2]) - 0.7 * abs(f[1]))
        plan.append((block, hops))
        for axis, dist, to in hops:
            wire = axis, dist > 0
            took = (to[2] - to[1]) * 16 / 46.5e3 + 0.03
            begin = max(when, free.get(wire, 0.0))
            free[wire] = begin + took * abs(dist)
            count += 1
            heapq.heappush(heap, (begin + took + 1.4 + 0.7 * abs(dist), count, to))
    return plan


def iota(shape, dim):
    return lax.broadcasted_iota(jnp.int32, shape, dim)


def kernel(
    images_h, refs_h, shifts_h, owners_h, rows_h, interp_h, reg_h,
    vol, res,
    images, refs, shifts, owners, slot_rows, interp, reg,
    gat, rot, cos_t, sin_t, acc, wts, part, own_tot, pair_s, pair_r, z_s, z_r,
    meta_s, meta_r, stat_s, stat_r, mz_s, mz_r, mb_s, mb_r, val_s, val_r, rep_s, rep_r,
    oh, oh_t, scat, scat_t, cnt,
    loc_sem, gat_send, gat_recv, pair_send, pair_recv, z_send, z_recv, sends, recvs, token,
):
    me_i, me_o = lax.axis_index("img"), lax.axis_index("ori")
    x, y = me_o // NY, lax.rem(me_o, NY)
    z, c = me_i // 2, lax.rem(me_i, 2)
    up, down = lax.rem(z + 1, NZ) * 2 + c, lax.rem(z + NZ - 1, NZ) * 2 + c

    def along(axis, dist):
        if axis == "x":
            return lax.rem(x + NX + dist, NX) * NY + y
        return x * NY + lax.rem(y + NY + dist, NY)

    plan = gather_plan()
    number = {block: i for i, (block, _) in enumerate(plan)}
    near = sorted({(axis, dist) for _, hops in plan for axis, dist, _ in hops})
    barrier = pltpu.get_barrier_semaphore()
    for axis, dist in near:
        pl.semaphore_signal(barrier, 1, device_id={"ori": along(axis, dist)}, device_id_type=MESH)
    for to in (up, down, z * 2 + 1 - c):
        pl.semaphore_signal(barrier, 1, device_id={"img": to}, device_id_type=MESH)

    loads = [
        pltpu.make_async_copy(src, dst, loc_sem.at[i])
        for i, (src, dst) in enumerate(
            [(images_h, images), (shifts_h, shifts), (refs_h, refs), (owners_h, owners), (rows_h, slot_rows),
             (interp_h, interp), (reg_h, reg)]
        )
    ]
    for copy in loads:
        copy.start()

    loads[0].wait()
    gat[me_o] = jnp.concatenate(
        [images[:, q * QUART : (q + 1) * QUART].astype(F32) for q in range(4)], axis=0
    ).astype(BF16)
    loads[1].wait()

    unit = 2.0 * math.pi / 128.0
    eye12 = iota((SHIFTS, SHIFTS), 0) == iota((SHIFTS, SHIFTS), 1)
    step_x = unit * jnp.sum(jnp.where(eye12, shifts[0:1, :], 0.0), axis=1, keepdims=True)
    step_y = unit * jnp.sum(jnp.where(eye12, shifts[1:2, :], 0.0), axis=1, keepdims=True)

    def tables(step):
        lane12 = iota((SHIFTS, 128), 1)
        base = step_x * (lane12 % 64).astype(F32) + step_y * (lane12 // 64).astype(F32)
        tile = step_y * (2 * lane12 - 64).astype(F32)
        base_c, base_s, tile_c, tile_s = jnp.cos(base), jnp.sin(base), jnp.cos(tile), jnp.sin(tile)
        for t in range(64):
            half, col = t // 32, (t % 32) * 128
            tc, ts = tile_c[:, t : t + 1], tile_s[:, t : t + 1]
            cos_t[half, :, col : col + 128] = base_c * tc - base_s * ts
            sin_t[half, :, col : col + 128] = base_s * tc + base_c * ts

    def rotate(step):
        if step == 0:
            loads[2].wait()
        col = step * 256
        for half in range(2):
            real = refs[:, half * QUART + col : half * QUART + col + 256].astype(F32)
            imag = refs[:, (2 + half) * QUART + col : (2 + half) * QUART + col + 256].astype(F32)
            for s in range(SHIFTS):
                cs, sn = cos_t[half, s : s + 1, col : col + 256], sin_t[half, s : s + 1, col : col + 256]
                rot[half * 192 + s * 16 : half * 192 + s * 16 + 16, col : col + 256] = (
                    real * cs - imag * sn
                ).astype(BF16)
                rot[(2 + half) * 192 + s * 16 : (2 + half) * 192 + s * 16 + 16, col : col + 256] = (
                    real * sn + imag * cs
                ).astype(BF16)

    def routing(step):
        loads[3].wait()
        loads[4].wait()
        eye = iota((128, 128), 0) == iota((128, 128), 1)
        row_col = jnp.sum(jnp.where(eye, slot_rows[...].astype(F32), 0.0), axis=1, keepdims=True)
        own_col = jnp.sum(jnp.where(eye, owners[...].astype(F32), 0.0), axis=1, keepdims=True)
        blocks = [(q * 32 + u * 8) for u in range(4) for q in range(4)]
        row_col = jnp.concatenate([row_col[b : b + 8] for b in blocks], axis=0)
        own_col = jnp.concatenate([own_col[b : b + 8] for b in blocks], axis=0)
        lane128 = iota((128, 128), 1).astype(F32)
        owner_hot = (own_col == lane128).astype(F32)
        before = (iota((128, 128), 1) < iota((128, 128), 0)).astype(BF16)
        counts = jnp.dot(before, owner_hot.astype(BF16), preferred_element_type=F32)
        rank_col = jnp.sum(counts * owner_hot, axis=1, keepdims=True)
        slot_col = own_col * CAP + rank_col
        slot_row = jnp.sum(jnp.where(eye, slot_col, 0.0), axis=0, keepdims=True)
        oh[...] = (slot_row == iota((SLOTS, 128), 0).astype(F32)).astype(BF16)
        oh_t[...] = (slot_col == iota((128, SLOTS), 1).astype(F32)).astype(BF16)
        rank_rows = jnp.where(rank_col == lane128, row_col + 1.0, 0.0).astype(BF16)
        table = lax.dot_general(
            owner_hot.astype(BF16), rank_rows, (((0,), (0,)), ((), ())), preferred_element_type=F32
        ) - 1.0
        for d in range(N_ORI):
            meta_s[d] = table[d : d + 1, :]

    def pass_token(step):
        if step:
            for way in range(2):
                pl.semaphore_wait(token.at[step - 1, way], 1)
        if step < 4:
            for way, to in enumerate((up, down)):
                pl.semaphore_signal(token.at[step, way], 1, device_id={"img": to}, device_id_type=MESH)

    pl.semaphore_wait(barrier, len(near) + 3)

    def gather_copy(block, dx, dy, to):
        src = lax.rem(x + NX - dx, NX) * NY + lax.rem(y + NY - dy, NY)
        ref = gat.at[src, :, pl.ds(block[1], block[2] - block[1])]
        return pltpu.make_async_remote_copy(
            src_ref=ref, dst_ref=ref, send_sem=gat_send, recv_sem=gat_recv.at[number[block]],
            device_id={"ori": to}, device_id_type=MESH,
        )

    def spread(send_ref, recv_ref, which):
        def one(p, carry):
            to = lax.rem(me_o + p, N_ORI)
            src = send_ref.at[0] if send_ref.shape[0] == 1 else send_ref.at[to]
            pltpu.make_async_remote_copy(
                src_ref=src, dst_ref=recv_ref.at[me_o], send_sem=sends.at[which], recv_sem=recvs.at[which],
                device_id={"ori": to}, device_id_type=MESH,
            ).start()
            return carry

        lax.fori_loop(1, N_ORI, one, 0)

    def await_bytes(ref, sem):
        pltpu.make_async_copy(ref, ref, sem).wait()

    jobs = [(pass_token, 0), (tables, 0)]
    jobs += [(rotate, i) for i in range(QUART // 256)]
    jobs[6:6] = [(pass_token, 1)]
    jobs[10:10] = [(pass_token, 2)]
    jobs[14:14] = [(pass_token, 3)]
    jobs += [(pass_token, 4), (routing, 0)]
    due = [2 + i * (len(plan) - 8) // len(jobs) for i in range(len(jobs))]
    for i, (block, hops) in enumerate(plan):
        dx, dy = block[3:5]
        if dx or dy:
            gather_copy(block, dx, dy, me_o).wait_recv()
        for axis, dist, to in hops:
            gather_copy(to, dx, dy, along(axis, dist)).start()
        while due and due[0] <= i:
            due.pop(0)
            job, step = jobs.pop(0)
            job(step)
    for job, step in jobs:
        job(step)
    spread(meta_s, meta_r, 0)
    meta_r[me_o] = meta_s[me_o]

    def score(step, carry):
        cols = pl.ds(step * SCORE_COLS if isinstance(step, int) else pl.multiple_of(step * SCORE_COLS, SCORE_COLS), SCORE_COLS)
        block = gat[:, :, cols].reshape(N_ORI * 8, SCORE_COLS)
        got = lax.dot_general(rot[:, cols], block, (((1,), (1,)), ((), ())), preferred_element_type=F32)
        acc[...] = got if isinstance(step, int) else acc[...] + got
        return carry

    score(0, 0)
    if QUART > SCORE_COLS:
        lax.fori_loop(1, QUART // SCORE_COLS, score, 0)

    lane = iota((192, 256), 1)
    quarter = lane % 8 // 2
    mine = jnp.zeros((192, 256), F32)
    for q in range(4):
        mine = mine + jnp.where(quarter == q, acc[q * 192 : (q + 1) * 192, :], 0.0)
    left, right = iota((256, 256), 0), iota((256, 256), 1)
    fold = ((left // 8 == right // 8) & (left % 2 == right % 2)).astype(F32)
    scores = jnp.dot(mine, fold, precision=HIGH, preferred_element_type=F32) * (2.0 / math.sqrt(COEF))
    peak = jnp.max(scores, axis=0, keepdims=True)
    expo = jnp.exp(scores - peak)
    total = jnp.sum(expo, axis=0, keepdims=True)
    stat = jnp.where(iota((1, 256), 1) // 2 % 2 == 0, peak, total)
    stat_s[0] = stat
    spread(stat_s, stat_r, 1)
    stat_r[me_o] = stat

    await_bytes(meta_r.at[pl.ds(0, N_ORI - 1)], recvs.at[0])
    rep = (iota((SLOTS, N_ORI), 0) // CAP == iota((SLOTS, N_ORI), 1)).astype(BF16)
    rid = jnp.dot(rep, meta_r[...].reshape(N_ORI, 128).astype(BF16), preferred_element_type=F32)
    rid = jnp.where(iota((SLOTS, 128), 0) % CAP == iota((SLOTS, 128), 1), rid, 0.0)
    hot = (jnp.sum(rid, axis=1, keepdims=True) == iota((SLOTS, 128), 1).astype(F32)).astype(F32)
    scat_t[...] = hot.astype(BF16)
    scat[...] = jnp.transpose(hot).astype(BF16)
    cnt[...] = jnp.dot(scat[...], rep, preferred_element_type=F32)
    loads[6].wait()
    reg_col = jnp.sum(
        jnp.where(iota((ROWS, ROWS), 0) == iota((ROWS, ROWS), 1), reg[...], 0.0), axis=1, keepdims=True
    )

    loads[5].wait()
    await_bytes(stat_r.at[pl.ds(0, N_ORI - 1)], recvs.at[1])
    stats = stat_r[...].reshape(N_ORI, 256)
    even = iota((N_ORI, 256), 1) // 2 % 2 == 0
    peaks = jnp.where(even, stats, pltpu.roll(stats, 2, 1))
    totals = jnp.where(even, pltpu.roll(stats, 254, 1), stats)
    top = jnp.max(peaks, axis=0, keepdims=True)
    whole = jnp.sum(totals * jnp.exp(peaks - top), axis=0, keepdims=True)
    weights = expo * (jnp.exp(peak - top) / whole)
    for q in range(4):
        wts[q * 192 : (q + 1) * 192, :] = jnp.where(quarter == q, weights, 0.0).astype(BF16)

    mass = jnp.sum(jnp.where(quarter == 0, weights, 0.0), axis=1, keepdims=True)
    mass16 = mass[0:16]
    for s in range(1, SHIFTS):
        mass16 = mass16 + mass[s * 16 : s * 16 + 16]
    mass16 = jnp.broadcast_to(mass16, (16, 128))
    for o in range(N_IMG):
        mz_s[o] = mass16[o : o + 1, :]

    def send_mass(p, carry):
        to = lax.rem(me_i + p, N_IMG)
        pltpu.make_async_remote_copy(
            src_ref=mz_s.at[to], dst_ref=mz_r.at[me_i], send_sem=sends.at[2], recv_sem=recvs.at[2],
            device_id={"img": to}, device_id_type=MESH,
        ).start()
        return carry

    lax.fori_loop(1, N_IMG, send_mass, 0)
    mz_r[me_i] = mz_s[me_i]

    def pair_copy(u):
        return pltpu.make_async_remote_copy(
            src_ref=pair_s.at[u], dst_ref=pair_r.at[u], send_sem=pair_send.at[u], recv_sem=pair_recv.at[u],
            device_id={"img": z * 2 + 1 - c}, device_id_type=MESH,
        )

    def project(u, carry):
        for v in range(4):
            cols = pl.ds(pl.multiple_of(u * 1024 + v * 256, 256), 256)
            block = gat[:, :, cols].reshape(N_ORI * 8, 256)
            prod = jnp.dot(wts[...], block, preferred_element_type=F32)
            for half in range(2):
                re = jnp.zeros((16, 256), F32)
                im = jnp.zeros((16, 256), F32)
                for s in range(SHIFTS):
                    cs, sn = cos_t[half, s : s + 1, cols], sin_t[half, s : s + 1, cols]
                    sr = prod[half * 192 + s * 16 : half * 192 + s * 16 + 16, :]
                    si = prod[(2 + half) * 192 + s * 16 : (2 + half) * 192 + s * 16 + 16, :]
                    re = re + sr * cs + si * sn
                    im = im - sr * sn + si * cs
                for a in range(2):
                    part[u, :, half * 8 + v * 2 + a, :] = re[:, a * 128 : a * 128 + 128]
                    part[u, :, (2 + half) * 8 + v * 2 + a, :] = im[:, a * 128 : a * 128 + 128]
        for k in range(NZ):
            pair_s[u, k] = part[u, 2 * k + 1 - c].astype(BF16)
        pair_copy(u).start()
        return carry

    def reduce_pair(u):
        pair_copy(u).wait_recv()
        own_tot[u] = part[u, 2 * z + c] + pair_r[u, z].astype(F32)
        for p in (4, 3, 5, 2, 6, 1, 7):
            to = lax.rem(z + p, NZ)
            z_s[u, to] = (part[u, 2 * to + c] + pair_r[u, to].astype(F32)).astype(BF16)
            pltpu.make_async_remote_copy(
                src_ref=z_s.at[u, to], dst_ref=z_r.at[u, z], send_sem=z_send.at[u], recv_sem=z_recv.at[u],
                device_id={"img": to * 2 + c}, device_id_type=MESH,
            ).start()

    def project_and_reduce(u, carry):
        project(u, 0)
        reduce_pair(u - 1)
        return carry

    project(0, 0)
    lax.fori_loop(1, 4, project_and_reduce, 0)
    reduce_pair(3)

    await_bytes(mz_r.at[pl.ds(0, N_IMG - 1)], recvs.at[2])
    mass_all = jnp.sum(mz_r[...].reshape(N_IMG, 128), axis=0, keepdims=True)
    mb_s[0] = mass_all
    spread(mb_s, mb_r, 3)
    mb_r[me_o] = mass_all

    sums = []
    for u in range(4):
        await_bytes(z_r.at[u, pl.ds(0, NZ - 1)], z_recv.at[u])
        tot = own_tot[u]
        for p in range(1, NZ):
            tot = tot + z_r[u, lax.rem(z + p, NZ)].astype(F32)
        sums.append(tot)
    segments = jnp.concatenate(sums, axis=0).astype(BF16)

    val_s[...] = jnp.dot(oh[...], segments, preferred_element_type=F32).astype(BF16).reshape(N_ORI, CAP, 128)
    spread(val_s, val_r, 4)
    val_r[me_o] = val_s[me_o]

    await_bytes(mb_r.at[pl.ds(0, N_ORI - 1)], recvs.at[3])
    weight_sum = jnp.dot(
        cnt[0:ROWS, :], mb_r[...].reshape(N_ORI, 128), precision=HIGH, preferred_element_type=F32
    )
    denom = weight_sum + reg_col

    await_bytes(val_r.at[pl.ds(0, N_ORI - 1)], recvs.at[4])
    inserted = jnp.dot(scat[0:ROWS, :], val_r[...].reshape(SLOTS, 128), preferred_element_type=F32)
    mapped = jnp.dot(inserted, interp[...], precision=HIGH, preferred_element_type=F32)
    volume = mapped / denom
    vol[...] = volume
    back = lax.dot_general(
        volume, interp[...], (((1,), (1,)), ((), ())), precision=HIGH, preferred_element_type=F32
    )
    reply = jnp.dot(scat_t[:, 0:ROWS], back.astype(BF16), preferred_element_type=F32)
    rep_s[...] = reply.astype(BF16).reshape(N_ORI, CAP, 128)
    spread(rep_s, rep_r, 5)
    rep_r[me_o] = rep_s[me_o]

    await_bytes(gat.at[pl.ds(0, N_ORI - 1)], gat_send)
    for u in range(4):
        pair_copy(u).wait_send()
        await_bytes(z_s.at[u, pl.ds(0, NZ - 1)], z_send.at[u])
    await_bytes(meta_s.at[pl.ds(0, N_ORI - 1)], sends.at[0])
    await_bytes(stat_r.at[pl.ds(0, N_ORI - 1)], sends.at[1])
    await_bytes(mz_s.at[pl.ds(0, N_IMG - 1)], sends.at[2])
    await_bytes(mb_r.at[pl.ds(0, N_ORI - 1)], sends.at[3])
    await_bytes(val_s.at[pl.ds(0, N_ORI - 1)], sends.at[4])

    await_bytes(rep_r.at[pl.ds(0, N_ORI - 1)], recvs.at[5])
    picked = jnp.dot(oh_t[...], rep_r[...].reshape(SLOTS, 128), preferred_element_type=F32)
    for u in range(4):
        for q in range(4):
            res[q * 32 + u * 8 : q * 32 + u * 8 + 8, :] = picked[u * 32 + q * 8 : u * 32 + q * 8 + 8, :]
    await_bytes(rep_s.at[pl.ds(0, N_ORI - 1)], sends.at[5])


def shards(images, references, shifts, owners, slot_rows, interpolation, regularizer):
    vmem = pl.BlockSpec(memory_space=pltpu.VMEM)
    anywhere = pl.BlockSpec(memory_space=pl.ANY)
    volume, resampled = pl.pallas_call(
        kernel,
        out_shape=(jax.ShapeDtypeStruct((ROWS, 128), F32), jax.ShapeDtypeStruct((128, 128), F32)),
        in_specs=[anywhere] * 7,
        out_specs=(vmem, vmem),
        scratch_shapes=[
            pltpu.VMEM((2, COEF), BF16),
            pltpu.VMEM((16, COEF), BF16),
            pltpu.VMEM((2, SHIFTS), F32),
            pltpu.VMEM((1, 128), jnp.int32),
            pltpu.VMEM((1, 128), jnp.int32),
            pltpu.VMEM((128, 128), F32),
            pltpu.VMEM((1, ROWS), F32),
            pltpu.VMEM((N_ORI, 8, QUART), BF16),
            pltpu.VMEM((768, QUART), BF16),
            pltpu.VMEM((2, SHIFTS, QUART), F32),
            pltpu.VMEM((2, SHIFTS, QUART), F32),
            pltpu.VMEM((768, 256), F32),
            pltpu.VMEM((768, 256), BF16),
            pltpu.VMEM((4, N_IMG, 32, 128), F32),
            pltpu.VMEM((4, 32, 128), F32),
            pltpu.VMEM((4, NZ, 32, 128), BF16),
            pltpu.VMEM((4, NZ, 32, 128), BF16),
            pltpu.VMEM((4, NZ, 32, 128), BF16),
            pltpu.VMEM((4, NZ, 32, 128), BF16),
            pltpu.VMEM((N_ORI, 1, 128), F32),
            pltpu.VMEM((N_ORI, 1, 128), F32),
            pltpu.VMEM((1, 1, 256), F32),
            pltpu.VMEM((N_ORI, 1, 256), F32),
            pltpu.VMEM((N_IMG, 1, 128), F32),
            pltpu.VMEM((N_IMG, 1, 128), F32),
            pltpu.VMEM((1, 1, 128), F32),
            pltpu.VMEM((N_ORI, 1, 128), F32),
            pltpu.VMEM((N_ORI, CAP, 128), BF16),
            pltpu.VMEM((N_ORI, CAP, 128), BF16),
            pltpu.VMEM((N_ORI, CAP, 128), BF16),
            pltpu.VMEM((N_ORI, CAP, 128), BF16),
            pltpu.VMEM((SLOTS, 128), BF16),
            pltpu.VMEM((128, SLOTS), BF16),
            pltpu.VMEM((128, SLOTS), BF16),
            pltpu.VMEM((SLOTS, 128), BF16),
            pltpu.VMEM((128, N_ORI), F32),
            pltpu.SemaphoreType.DMA((7,)),
            pltpu.SemaphoreType.DMA,
            pltpu.SemaphoreType.DMA((len(gather_plan()),)),
            pltpu.SemaphoreType.DMA((4,)),
            pltpu.SemaphoreType.DMA((4,)),
            pltpu.SemaphoreType.DMA((4,)),
            pltpu.SemaphoreType.DMA((4,)),
            pltpu.SemaphoreType.DMA((6,)),
            pltpu.SemaphoreType.DMA((6,)),
            pltpu.SemaphoreType.REGULAR((4, 2)),
        ],
        compiler_params=pltpu.CompilerParams(
            collective_id=0, has_side_effects=True, vmem_limit_bytes=60 * 1024 * 1024
        ),
    )(
        images,
        references,
        shifts.T,
        owners.reshape(1, 128),
        slot_rows.reshape(1, 128),
        interpolation,
        regularizer.reshape(1, ROWS),
    )
    return (volume, resampled.reshape(1, COEF))


def solution(mesh):
    in_specs = (
        P(("img", "ori"), None),
        P("ori", None),
        P(),
        P(("ori", "img"), None),
        P(("ori", "img")),
        P(("ori", "img"), None),
        P(("ori", "img")),
    )
    out_specs = (P(("ori", "img"), None), P(("ori", "img"), None))
    return jax.shard_map(shards, mesh=mesh, in_specs=in_specs, out_specs=out_specs, check_vma=False)
```

```python
import heapq
import math

import jax
import jax.numpy as jnp
from jax import lax
from jax.experimental import pallas as pl
from jax.experimental.pallas import tpu as pltpu
from jax.sharding import PartitionSpec as P

NX, NY, NZ = 4, 8, 8
N_ORI = NX * NY
N_IMG = 2 * NZ
COEF = 16384
QUART = COEF // 4
SHIFTS = 12
CAP = 16
SLOTS = N_ORI * CAP
ROWS = 64
MESH = pl.DeviceIdType.MESH
SCORE_COLS = 2048
HIGH = lax.Precision.HIGHEST
F32, BF16 = jnp.float32, jnp.bfloat16

SPLIT = 1536
RANGE = {"A": (0, SPLIT), "B": (SPLIT, QUART)}
PARENT = {"A": ((0, 0, 1), (0, 0, 1, 2, 2)), "B": ((0, 0, 1), (0, 0, 0, 2, 2))}


def ring_steps(parents, size, d, sign, lo, hi, mid):
    for k in range(1, size // 2 + 1):
        for way in (1, -1):
            if d != way * parents[k] % size or d and sign != way:
                continue
            a, b = lo, hi
            if k == size // 2:
                a, b = (lo, min(hi, mid)) if way > 0 else (max(lo, mid), hi)
            if a < b:
                yield way, way * k % size, k - parents[k], a, b


def forwards(block):
    route, lo, hi, dx, dy, sx, sy = block
    mid = sum(RANGE[route]) // 2
    par_x, par_y = PARENT[route]
    out = []
    if route == "A" or dx == 0:
        for way, d, hops, a, b in ring_steps(par_y, NY, dy, sy, lo, hi, mid):
            out.append(("y", way * hops, (route, a, b, dx, d, sx, way)))
    if route == "B" or dy == 0:
        for way, d, hops, a, b in ring_steps(par_x, NX, dx, sx, lo, hi, mid):
            out.append(("x", way * hops, (route, a, b, d, dy, way, sy)))
    return out


def depth(block):
    return max((1.4 + 0.7 * abs(h) + depth(k) for _, h, k in forwards(block)), default=0)


def gather_plan():
    heap = [(0.0, i, (r, *RANGE[r], 0, 0, 0, 0)) for i, r in enumerate("BA")]
    free, plan, count = {}, [], 10
    while heap:
        when, _, block = heapq.heappop(heap)
        hops = sorted(forwards(block), key=lambda f: -depth(f[2]) - 0.7 * abs(f[1]))
        plan.append((block, hops))
        for axis, dist, to in hops:
            wire = axis, dist > 0
            took = (to[2] - to[1]) * 16 / 46.5e3 + 0.03
            begin = max(when, free.get(wire, 0.0))
            free[wire] = begin + took * abs(dist)
            count += 1
            heapq.heappush(heap, (begin + took + 1.4 + 0.7 * abs(dist), count, to))
    return plan


def row(half, s, part):
    return ((half * SHIFTS + s) * 2 + part) * 16


def iota(shape, dim):
    return lax.broadcasted_iota(jnp.int32, shape, dim)


def kernel(
    images_h, refs_h, shifts_h, owners_h, rows_h, interp_h, reg_h,
    out,
    images, refs, shifts, owners, slot_rows, interp, reg,
    gat, rot, cos_t, sin_t, acc, wts, part, own_tot, pair_s, pair_r, z_s, z_r, relay_r,
    meta_s, meta_r, stat_s, stat_r, mz_s, mz_r, mb_s, mb_r, val_s, val_r, rep_s, rep_r,
    oh, oh_t, scat, scat_t, cnt,
    loc_sem, gat_send, gat_recv, pair_send, pair_recv, z_send, z_recv, sends, recvs, token,
):
    me_i, me_o = lax.axis_index("img"), lax.axis_index("ori")
    x, y = me_o // NY, lax.rem(me_o, NY)
    z, c = me_i // 2, lax.rem(me_i, 2)
    up, down = lax.rem(z + 1, NZ) * 2 + c, lax.rem(z + NZ - 1, NZ) * 2 + c

    def along(axis, dist):
        if axis == "x":
            return lax.rem(x + NX + dist, NX) * NY + y
        return x * NY + lax.rem(y + NY + dist, NY)

    plan = gather_plan()
    number = {block: i for i, (block, _) in enumerate(plan)}
    near = sorted({(axis, dist) for _, hops in plan for axis, dist, _ in hops})
    barrier = pltpu.get_barrier_semaphore()
    for axis, dist in near:
        pl.semaphore_signal(barrier, 1, device_id={"ori": along(axis, dist)}, device_id_type=MESH)
    for to in (up, down, z * 2 + 1 - c):
        pl.semaphore_signal(barrier, 1, device_id={"img": to}, device_id_type=MESH)

    loads = [
        pltpu.make_async_copy(src, dst, loc_sem.at[i])
        for i, (src, dst) in enumerate(
            [(images_h, images), (shifts_h, shifts), (refs_h, refs), (owners_h, owners), (rows_h, slot_rows),
             (interp_h, interp), (reg_h, reg)]
        )
    ]
    for copy in loads:
        copy.start()

    loads[0].wait()
    gat[me_o] = jnp.concatenate(
        [images[:, q * QUART : (q + 1) * QUART].astype(F32) for q in range(4)], axis=0
    ).astype(BF16)
    loads[1].wait()

    unit = 2.0 * math.pi / 128.0
    eye12 = iota((SHIFTS, SHIFTS), 0) == iota((SHIFTS, SHIFTS), 1)
    step_x = unit * jnp.sum(jnp.where(eye12, shifts[0:1, :], 0.0), axis=1, keepdims=True)
    step_y = unit * jnp.sum(jnp.where(eye12, shifts[1:2, :], 0.0), axis=1, keepdims=True)

    def tables(step):
        lane12 = iota((SHIFTS, 128), 1)
        base = step_x * (lane12 % 64).astype(F32) + step_y * (lane12 // 64).astype(F32)
        tile = step_y * (2 * lane12 - 64).astype(F32)
        base_c, base_s, tile_c, tile_s = jnp.cos(base), jnp.sin(base), jnp.cos(tile), jnp.sin(tile)
        for t in range(64):
            half, col = t // 32, (t % 32) * 128
            tc, ts = tile_c[:, t : t + 1], tile_s[:, t : t + 1]
            cos_t[half, :, col : col + 128] = base_c * tc - base_s * ts
            sin_t[half, :, col : col + 128] = base_s * tc + base_c * ts

    def rotate(step):
        if step == 0:
            loads[2].wait()
        col = step * 256
        for half in range(2):
            real = refs[:, half * QUART + col : half * QUART + col + 256].astype(F32)
            imag = refs[:, (2 + half) * QUART + col : (2 + half) * QUART + col + 256].astype(F32)
            for s in range(SHIFTS):
                cs, sn = cos_t[half, s : s + 1, col : col + 256], sin_t[half, s : s + 1, col : col + 256]
                r = row(half, s, 0)
                rot[r : r + 16, col : col + 256] = (real * cs - imag * sn).astype(BF16)
                rot[r + 16 : r + 32, col : col + 256] = (real * sn + imag * cs).astype(BF16)

    def routing(step):
        loads[3].wait()
        loads[4].wait()
        eye = iota((128, 128), 0) == iota((128, 128), 1)
        row_col = jnp.sum(jnp.where(eye, slot_rows[...].astype(F32), 0.0), axis=1, keepdims=True)
        own_col = jnp.sum(jnp.where(eye, owners[...].astype(F32), 0.0), axis=1, keepdims=True)
        blocks = [(q * 32 + u * 8) for u in range(4) for q in range(4)]
        row_col = jnp.concatenate([row_col[b : b + 8] for b in blocks], axis=0)
        own_col = jnp.concatenate([own_col[b : b + 8] for b in blocks], axis=0)
        lane128 = iota((128, 128), 1).astype(F32)
        owner_hot = (own_col == lane128).astype(F32)
        before = (iota((128, 128), 1) < iota((128, 128), 0)).astype(BF16)
        counts = jnp.dot(before, owner_hot.astype(BF16), preferred_element_type=F32)
        rank_col = jnp.sum(counts * owner_hot, axis=1, keepdims=True)
        slot_col = own_col * CAP + rank_col
        slot_row = jnp.sum(jnp.where(eye, slot_col, 0.0), axis=0, keepdims=True)
        oh[...] = (slot_row == iota((SLOTS, 128), 0).astype(F32)).astype(BF16)
        oh_t[...] = (slot_col == iota((128, SLOTS), 1).astype(F32)).astype(BF16)
        rank_rows = jnp.where(rank_col == lane128, row_col + 1.0, 0.0).astype(BF16)
        table = lax.dot_general(
            owner_hot.astype(BF16), rank_rows, (((0,), (0,)), ((), ())), preferred_element_type=F32
        ) - 1.0
        for d in range(N_ORI):
            meta_s[d] = table[d : d + 1, :]

    def pass_token(step):
        if step:
            for way in range(2):
                pl.semaphore_wait(token.at[step - 1, way], 1)
        if step < 4:
            for way, to in enumerate((up, down)):
                pl.semaphore_signal(token.at[step, way], 1, device_id={"img": to}, device_id_type=MESH)

    pl.semaphore_wait(barrier, len(near) + 3)

    def gather_copy(block, dx, dy, to):
        src = lax.rem(x + NX - dx, NX) * NY + lax.rem(y + NY - dy, NY)
        ref = gat.at[src, :, pl.ds(block[1], block[2] - block[1])]
        return pltpu.make_async_remote_copy(
            src_ref=ref, dst_ref=ref, send_sem=gat_send, recv_sem=gat_recv.at[number[block]],
            device_id={"ori": to}, device_id_type=MESH,
        )

    xs = [lax.rem(x + d, NX) * NY for d in range(NX)]
    ys = [lax.rem(y + d, NY) for d in range(NY)]
    others = sorted(
        ((a, b) for a in range(NX) for b in range(NY) if a or b), key=lambda p: -min(p[0], NX - p[0]) - min(p[1], NY - p[1])
    )

    def spread(send_ref, recv_ref, which):
        for a, b in others:
            to = xs[a] + ys[b]
            src = send_ref.at[0] if send_ref.shape[0] == 1 else send_ref.at[to]
            pltpu.make_async_remote_copy(
                src_ref=src, dst_ref=recv_ref.at[me_o], send_sem=sends.at[which], recv_sem=recvs.at[which],
                device_id={"ori": to}, device_id_type=MESH,
            ).start()

    def await_bytes(ref, sem):
        pltpu.make_async_copy(ref, ref, sem).wait()

    jobs = [(pass_token, 0), (tables, 0)]
    jobs += [(rotate, i) for i in range(QUART // 256)]
    jobs[6:6] = [(pass_token, 1)]
    jobs[10:10] = [(pass_token, 2)]
    jobs[14:14] = [(pass_token, 3)]
    jobs += [(pass_token, 4), (routing, 0)]
    due = [2 + i * (len(plan) - 8) // len(jobs) for i in range(len(jobs))]
    for i, (block, hops) in enumerate(plan):
        dx, dy = block[3:5]
        if dx or dy:
            gather_copy(block, dx, dy, me_o).wait_recv()
        for axis, dist, to in hops:
            gather_copy(to, dx, dy, along(axis, dist)).start()
        while due and due[0] <= i:
            due.pop(0)
            job, step = jobs.pop(0)
            job(step)
    for job, step in jobs:
        job(step)
    for h in range(2):
        acc[h * 384 : h * 384 + 384, :] = lax.dot_general(
            rot[h * 384 : h * 384 + 384, :], gat[...].reshape(N_ORI * 8, QUART), (((1,), (1,)), ((), ())),
            preferred_element_type=F32)

    quarter = iota((16, 256), 1) % 8 // 2
    places = [(half, im) for half in range(2) for im in range(2)]
    mine = []
    for s in range(SHIFTS):
        mine.append(
            sum(
                jnp.where(quarter == 2 * im + half, acc[row(half, s, im) : row(half, s, im) + 16, :], 0.0)
                for half, im in places
            )
        )
    mine = jnp.concatenate(mine, axis=0)
    left, right = iota((256, 256), 0), iota((256, 256), 1)
    fold = ((left // 8 == right // 8) & (left % 2 == right % 2)).astype(F32)
    scores = jnp.dot(mine, fold, precision=HIGH, preferred_element_type=F32) * (2.0 / math.sqrt(COEF))
    peak = jnp.max(scores, axis=0, keepdims=True)
    expo = jnp.exp(scores - peak)
    total = jnp.sum(expo, axis=0, keepdims=True)
    stat = jnp.where(iota((1, 256), 1) // 2 % 2 == 0, peak, total)
    stat_s[0] = stat
    spread(stat_s, stat_r, 1)
    stat_r[me_o] = stat
    spread(meta_s, meta_r, 0)
    meta_r[me_o] = meta_s[me_o]
    loads[5].wait()
    loads[6].wait()

    await_bytes(stat_r.at[pl.ds(0, N_ORI - 1)], recvs.at[1])
    stats = stat_r[...].reshape(N_ORI, 256)
    even = iota((N_ORI, 256), 1) // 2 % 2 == 0
    peaks = jnp.where(even, stats, pltpu.roll(stats, 2, 1))
    totals = jnp.where(even, pltpu.roll(stats, 254, 1), stats)
    top = jnp.max(peaks, axis=0, keepdims=True)
    whole = jnp.sum(totals * jnp.exp(peaks - top), axis=0, keepdims=True)
    weights = expo * (jnp.exp(peak - top) / whole)
    for s in range(SHIFTS):
        for half, im in places:
            r = row(half, s, im)
            wts[r : r + 16, :] = jnp.where(quarter == 2 * im + half, weights[s * 16 : s * 16 + 16], 0.0).astype(BF16)

    mass16 = weights[0:16]
    for s in range(1, SHIFTS):
        mass16 = mass16 + weights[s * 16 : s * 16 + 16]
    mass16 = jnp.sum(jnp.where(quarter == 0, mass16, 0.0), axis=1, keepdims=True)
    mass16 = jnp.broadcast_to(mass16, (16, 128))
    for o in range(N_IMG):
        mz_s[o] = mass16[o : o + 1, :]

    def send_mass(p, carry):
        to = lax.rem(me_i + p, N_IMG)
        pltpu.make_async_remote_copy(
            src_ref=mz_s.at[to], dst_ref=mz_r.at[me_i], send_sem=sends.at[2], recv_sem=recvs.at[2],
            device_id={"img": to}, device_id_type=MESH,
        ).start()
        return carry

    lax.fori_loop(1, N_IMG, send_mass, 0)
    mz_r[me_i] = mz_s[me_i]

    def pair_copy(u):
        return pltpu.make_async_remote_copy(
            src_ref=pair_s.at[u], dst_ref=pair_r.at[u], send_sem=pair_send.at[u], recv_sem=pair_recv.at[u],
            device_id={"img": z * 2 + 1 - c}, device_id_type=MESH,
        )

    def project(u):
        for v in range(2):
            col = u * 1024 + v * 512
            block = gat[:, :, col : col + 512].reshape(N_ORI * 8, 512)
            for half in range(2):
                prod = jnp.dot(wts[half * 384 : half * 384 + 384, :], block, preferred_element_type=F32)
                re = jnp.zeros((16, 512), F32)
                im = jnp.zeros((16, 512), F32)
                for s in range(SHIFTS):
                    cs, sn = cos_t[half, s : s + 1, col : col + 512], sin_t[half, s : s + 1, col : col + 512]
                    sr = prod[row(0, s, 0) : row(0, s, 0) + 16, :]
                    si = prod[row(0, s, 1) : row(0, s, 1) + 16, :]
                    re = re + sr * cs + si * sn
                    im = im - sr * sn + si * cs
                for a in range(4):
                    part[u, :, half * 8 + v * 4 + a, :] = re[:, a * 128 : a * 128 + 128]
                    part[u, :, (2 + half) * 8 + v * 4 + a, :] = im[:, a * 128 : a * 128 + 128]
        for k in range(NZ):
            pair_s[u, k] = part[u, 2 * k + 1 - c].astype(BF16)
        pair_copy(u).start()

    zs = [lax.rem(z + d, NZ) for d in range(NZ)]

    def chip_sum(u, to):
        return part[u, 2 * to + c] + pair_r[u, to].astype(F32)

    def z_copy(u, src, dst, dist, sem):
        return pltpu.make_async_remote_copy(
            src_ref=src, dst_ref=dst, send_sem=z_send.at[u], recv_sem=sem,
            device_id={"img": zs[dist % NZ] * 2 + c}, device_id_type=MESH,
        )

    def first_leg(u):
        pair_copy(u).wait_recv()
        own_tot[u] = chip_sum(u, z)
        if u == 3:
            for d in (4, 3, 5, 2, 6, 1, 7):
                z_s[u, d] = chip_sum(u, zs[d]).astype(BF16)
                z_copy(u, z_s.at[u, d], z_r.at[u, NZ - d], d, z_recv.at[u, 0]).start()
            return
        z_s[u, 4] = chip_sum(u, zs[4]).astype(BF16)
        for way, (far, via, near_by) in enumerate(((3, 1, 1), (5, 7, 7))):
            z_s[u, far] = chip_sum(u, zs[far]).astype(BF16)
            half = pl.ds(way * 16, 16)
            z_copy(u, z_s.at[u, 4, half], relay_r.at[u, 2 + way, half], 2 * via, z_recv.at[u, 3 + way]).start()
            z_copy(u, z_s.at[u, far], relay_r.at[u, way], via, z_recv.at[u, 1 + way]).start()
            z_s[u, near_by] = chip_sum(u, zs[near_by]).astype(BF16)
        for near_by in (1, 7):
            z_copy(u, z_s.at[u, near_by], z_r.at[u, NZ - near_by], near_by, z_recv.at[u, 0]).start()

    def second_leg(u):
        for way, (to, other) in enumerate(((2, 16), (6, 0))):
            await_bytes(relay_r.at[u, way], z_recv.at[u, 1 + way])
            half = pl.ds(way * 16, 16)
            await_bytes(relay_r.at[u, 2 + way, half], z_recv.at[u, 3 + way])
            total = chip_sum(u, zs[to]) + relay_r[u, way].astype(F32)
            far = relay_r[u, 2 + way, way * 16 : way * 16 + 16, :].astype(F32)
            zero = jnp.zeros((16, 128), F32)
            total = total + jnp.concatenate([zero, far] if way else [far, zero], axis=0)
            z_s[u, to] = total.astype(BF16)
            z_copy(u, z_s.at[u, to], z_r.at[u, NZ - to], to, z_recv.at[u, 0]).start()

    project(0)
    for u in range(1, 4):
        project(u)
        first_leg(u - 1)
    first_leg(3)
    for u in range(3):
        second_leg(u)

    await_bytes(mz_r.at[pl.ds(0, N_IMG - 1)], recvs.at[2])
    mass_all = jnp.sum(mz_r[...].reshape(N_IMG, 128), axis=0, keepdims=True)
    mb_s[0] = mass_all
    spread(mb_s, mb_r, 3)
    mb_r[me_o] = mass_all

    await_bytes(meta_r.at[pl.ds(0, N_ORI - 1)], recvs.at[0])
    rep = (iota((SLOTS, N_ORI), 0) // CAP == iota((SLOTS, N_ORI), 1)).astype(BF16)
    rid = jnp.dot(rep, meta_r[...].reshape(N_ORI, 128).astype(BF16), preferred_element_type=F32)
    rid = jnp.where(iota((SLOTS, 128), 0) % CAP == iota((SLOTS, 128), 1), rid, 0.0)
    hot = (jnp.sum(rid, axis=1, keepdims=True) == iota((SLOTS, 128), 1).astype(F32)).astype(F32)
    scat_t[...] = hot.astype(BF16)
    scat[...] = jnp.transpose(hot).astype(BF16)
    cnt[...] = jnp.dot(scat[...], rep, preferred_element_type=F32)
    reg_col = jnp.sum(
        jnp.where(iota((ROWS, ROWS), 0) == iota((ROWS, ROWS), 1), reg[...], 0.0), axis=1, keepdims=True
    )

    sums = []
    for u in range(4):
        sources = (1, 2, 6, 7) if u < 3 else range(1, NZ)
        await_bytes(z_r.at[u, pl.ds(0, len(sources))], z_recv.at[u, 0])
        tot = own_tot[u]
        for d in sources:
            tot = tot + z_r[u, d].astype(F32)
        sums.append(tot)
    segments = jnp.concatenate(sums, axis=0).astype(BF16)

    val_s[...] = jnp.dot(oh[...], segments, preferred_element_type=F32).astype(BF16).reshape(N_ORI, CAP, 128)
    spread(val_s, val_r, 4)
    val_r[me_o] = val_s[me_o]

    await_bytes(mb_r.at[pl.ds(0, N_ORI - 1)], recvs.at[3])
    weight_sum = jnp.dot(
        cnt[0:ROWS, :], mb_r[...].reshape(N_ORI, 128), precision=HIGH, preferred_element_type=F32
    )
    denom = weight_sum + reg_col

    await_bytes(val_r.at[pl.ds(0, N_ORI - 1)], recvs.at[4])
    inserted = jnp.dot(scat[0:ROWS, :], val_r[...].reshape(SLOTS, 128), preferred_element_type=F32)
    mapped = jnp.dot(inserted, interp[...], precision=HIGH, preferred_element_type=F32)
    volume = mapped / denom
    out[0:ROWS, :] = volume
    back = lax.dot_general(
        volume, interp[...], (((1,), (1,)), ((), ())), precision=HIGH, preferred_element_type=F32
    )
    reply = jnp.dot(scat_t[:, 0:ROWS], back.astype(BF16), preferred_element_type=F32)
    rep_s[...] = reply.astype(BF16).reshape(N_ORI, CAP, 128)
    spread(rep_s, rep_r, 5)
    rep_r[me_o] = rep_s[me_o]

    await_bytes(gat.at[pl.ds(0, N_ORI - 1)], gat_send)
    for u in range(4):
        pair_copy(u).wait_send()
        await_bytes(z_s.at[u, pl.ds(0, NZ - 1)], z_send.at[u])
    await_bytes(meta_s.at[pl.ds(0, N_ORI - 1)], sends.at[0])
    await_bytes(stat_r.at[pl.ds(0, N_ORI - 1)], sends.at[1])
    await_bytes(mz_s.at[pl.ds(0, N_IMG - 1)], sends.at[2])
    await_bytes(mb_r.at[pl.ds(0, N_ORI - 1)], sends.at[3])
    await_bytes(val_s.at[pl.ds(0, N_ORI - 1)], sends.at[4])

    await_bytes(rep_r.at[pl.ds(0, N_ORI - 1)], recvs.at[5])
    picked = jnp.dot(oh_t[...], rep_r[...].reshape(SLOTS, 128), preferred_element_type=F32)
    for u in range(4):
        for q in range(4):
            to = ROWS + q * 32 + u * 8
            out[to : to + 8, :] = picked[u * 32 + q * 8 : u * 32 + q * 8 + 8, :]
    await_bytes(rep_s.at[pl.ds(0, N_ORI - 1)], sends.at[5])


def hand_over(both, vol, res):
    vol[...] = both[0:ROWS, :]
    res[...] = both[ROWS : ROWS + 128, :]


def shards(images, references, shifts, owners, slot_rows, interpolation, regularizer):
    vmem = pl.BlockSpec(memory_space=pltpu.VMEM)
    anywhere = pl.BlockSpec(memory_space=pl.ANY)
    both = pl.pallas_call(
        kernel,
        out_shape=jax.ShapeDtypeStruct((ROWS + 128, 128), F32),
        in_specs=[anywhere] * 7,
        out_specs=vmem,
        scratch_shapes=[
            pltpu.VMEM((2, COEF), BF16),
            pltpu.VMEM((16, COEF), BF16),
            pltpu.VMEM((2, SHIFTS), F32),
            pltpu.VMEM((1, 128), jnp.int32),
            pltpu.VMEM((1, 128), jnp.int32),
            pltpu.VMEM((128, 128), F32),
            pltpu.VMEM((1, ROWS), F32),
            pltpu.VMEM((N_ORI, 8, QUART), BF16),
            pltpu.VMEM((768, QUART), BF16),
            pltpu.VMEM((2, SHIFTS, QUART), F32),
            pltpu.VMEM((2, SHIFTS, QUART), F32),
            pltpu.VMEM((768, 256), F32),
            pltpu.VMEM((768, 256), BF16),
            pltpu.VMEM((4, N_IMG, 32, 128), F32),
            pltpu.VMEM((4, 32, 128), F32),
            pltpu.VMEM((4, NZ, 32, 128), BF16),
            pltpu.VMEM((4, NZ, 32, 128), BF16),
            pltpu.VMEM((4, NZ, 32, 128), BF16),
            pltpu.VMEM((4, NZ, 32, 128), BF16),
            pltpu.VMEM((3, 4, 32, 128), BF16),
            pltpu.VMEM((N_ORI, 1, 128), F32),
            pltpu.VMEM((N_ORI, 1, 128), F32),
            pltpu.VMEM((1, 1, 256), F32),
            pltpu.VMEM((N_ORI, 1, 256), F32),
            pltpu.VMEM((N_IMG, 1, 128), F32),
            pltpu.VMEM((N_IMG, 1, 128), F32),
            pltpu.VMEM((1, 1, 128), F32),
            pltpu.VMEM((N_ORI, 1, 128), F32),
            pltpu.VMEM((N_ORI, CAP, 128), BF16),
            pltpu.VMEM((N_ORI, CAP, 128), BF16),
            pltpu.VMEM((N_ORI, CAP, 128), BF16),
            pltpu.VMEM((N_ORI, CAP, 128), BF16),
            pltpu.VMEM((SLOTS, 128), BF16),
            pltpu.VMEM((128, SLOTS), BF16),
            pltpu.VMEM((128, SLOTS), BF16),
            pltpu.VMEM((SLOTS, 128), BF16),
            pltpu.VMEM((128, N_ORI), F32),
            pltpu.SemaphoreType.DMA((7,)),
            pltpu.SemaphoreType.DMA,
            pltpu.SemaphoreType.DMA((len(gather_plan()),)),
            pltpu.SemaphoreType.DMA((4,)),
            pltpu.SemaphoreType.DMA((4,)),
            pltpu.SemaphoreType.DMA((4,)),
            pltpu.SemaphoreType.DMA((4, 5)),
            pltpu.SemaphoreType.DMA((6,)),
            pltpu.SemaphoreType.DMA((6,)),
            pltpu.SemaphoreType.REGULAR((4, 2)),
        ],
        compiler_params=pltpu.CompilerParams(
            collective_id=0, has_side_effects=True, vmem_limit_bytes=60 * 1024 * 1024
        ),
    )(
        images,
        references,
        shifts.T,
        owners.reshape(1, 128),
        slot_rows.reshape(1, 128),
        interpolation,
        regularizer.reshape(1, ROWS),
    )
    volume, resampled = pl.pallas_call(
        hand_over,
        out_shape=(jax.ShapeDtypeStruct((ROWS, 128), F32), jax.ShapeDtypeStruct((128, 128), F32)),
        in_specs=[vmem],
        out_specs=(vmem, vmem),
    )(both)
    return (volume, resampled.reshape(1, COEF))


def solution(mesh):
    in_specs = (
        P(("img", "ori"), None),
        P("ori", None),
        P(),
        P(("ori", "img"), None),
        P(("ori", "img")),
        P(("ori", "img"), None),
        P(("ori", "img")),
    )
    out_specs = (P(("ori", "img"), None), P(("ori", "img"), None))
    return jax.shard_map(shards, mesh=mesh, in_specs=in_specs, out_specs=out_specs, check_vma=False)
```

```python
import heapq
import math

import jax
import jax.numpy as jnp
from jax import lax
from jax.experimental import pallas as pl
from jax.experimental.pallas import tpu as pltpu
from jax.sharding import PartitionSpec as P

NX, NY, NZ = 4, 8, 8
N_ORI = NX * NY
N_IMG = 2 * NZ
COEF = 16384
QUART = COEF // 4
SHIFTS = 12
CAP = 16
SLOTS = N_ORI * CAP
ROWS = 64
MESH = pl.DeviceIdType.MESH
SCORE_COLS = 2048
HIGH = lax.Precision.HIGHEST
F32, BF16 = jnp.float32, jnp.bfloat16

SPLIT = 1536
RANGE = {"A": (0, SPLIT), "B": (SPLIT, QUART)}
PARENT = {"A": ((0, 0, 1), (0, 0, 1, 2, 2)), "B": ((0, 0, 1), (0, 0, 0, 2, 2))}


def ring_steps(parents, size, d, sign, lo, hi, mid):
    for k in range(1, size // 2 + 1):
        for way in (1, -1):
            if d != way * parents[k] % size or d and sign != way:
                continue
            a, b = lo, hi
            if k == size // 2:
                a, b = (lo, min(hi, mid)) if way > 0 else (max(lo, mid), hi)
            if a < b:
                yield way, way * k % size, k - parents[k], a, b


def forwards(block):
    route, lo, hi, dx, dy, sx, sy = block
    mid = sum(RANGE[route]) // 2
    par_x, par_y = PARENT[route]
    out = []
    if route == "A" or dx == 0:
        for way, d, hops, a, b in ring_steps(par_y, NY, dy, sy, lo, hi, mid):
            out.append(("y", way * hops, (route, a, b, dx, d, sx, way)))
    if route == "B" or dy == 0:
        for way, d, hops, a, b in ring_steps(par_x, NX, dx, sx, lo, hi, mid):
            out.append(("x", way * hops, (route, a, b, d, dy, way, sy)))
    return out


def depth(block):
    return max((1.4 + 0.7 * abs(h) + depth(k) for _, h, k in forwards(block)), default=0)


def gather_plan():
    heap = [(0.0, i, (r, *RANGE[r], 0, 0, 0, 0)) for i, r in enumerate("BA")]
    free, plan, count = {}, [], 10
    while heap:
        when, _, block = heapq.heappop(heap)
        hops = sorted(forwards(block), key=lambda f: -depth(f[2]) - 0.7 * abs(f[1]))
        plan.append((block, hops))
        for axis, dist, to in hops:
            wire = axis, dist > 0
            took = (to[2] - to[1]) * 16 / 46.5e3 + 0.03
            begin = max(when, free.get(wire, 0.0))
            free[wire] = begin + took * abs(dist)
            count += 1
            heapq.heappush(heap, (begin + took + 1.4 + 0.7 * abs(dist), count, to))
    return plan


def row(half, s, part):
    return ((half * SHIFTS + s) * 2 + part) * 16


def iota(shape, dim):
    return lax.broadcasted_iota(jnp.int32, shape, dim)


def kernel(
    images_h, refs_h, shifts_h, owners_h, rows_h, interp_h, reg_h,
    out,
    images, refs, shifts, owners, slot_rows, interp, reg,
    gat, rot, cos_t, sin_t, acc, wts, part, own_tot, pair_s, pair_r, z_s, z_r, relay_r,
    meta_s, meta_r, stat_s, stat_r, mz_s, mz_r, mb_s, mb_r, val_s, val_r, rep_s, rep_r,
    oh, oh_t, scat, scat_t, cnt,
    loc_sem, gat_send, gat_recv, pair_send, pair_recv, z_send, z_recv, sends, recvs, token,
):
    me_i, me_o = lax.axis_index("img"), lax.axis_index("ori")
    x, y = me_o // NY, lax.rem(me_o, NY)
    z, c = me_i // 2, lax.rem(me_i, 2)
    up, down = lax.rem(z + 1, NZ) * 2 + c, lax.rem(z + NZ - 1, NZ) * 2 + c

    def along(axis, dist):
        if axis == "x":
            return lax.rem(x + NX + dist, NX) * NY + y
        return x * NY + lax.rem(y + NY + dist, NY)

    plan = gather_plan()
    number = {block: i for i, (block, _) in enumerate(plan)}
    near = sorted({(axis, dist) for _, hops in plan for axis, dist, _ in hops})
    barrier = pltpu.get_barrier_semaphore()
    for axis, dist in near:
        pl.semaphore_signal(barrier, 1, device_id={"ori": along(axis, dist)}, device_id_type=MESH)
    for to in (up, down, z * 2 + 1 - c):
        pl.semaphore_signal(barrier, 1, device_id={"img": to}, device_id_type=MESH)

    loads = [
        pltpu.make_async_copy(src, dst, loc_sem.at[i])
        for i, (src, dst) in enumerate(
            [(images_h, images), (shifts_h, shifts), (refs_h, refs), (owners_h, owners), (rows_h, slot_rows),
             (interp_h, interp), (reg_h, reg)]
        )
    ]
    for copy in loads:
        copy.start()

    loads[0].wait()
    gat[me_o] = jnp.concatenate(
        [images[:, q * QUART : (q + 1) * QUART].astype(F32) for q in range(4)], axis=0
    ).astype(BF16)
    loads[1].wait()

    unit = 2.0 * math.pi / 128.0
    eye12 = iota((SHIFTS, SHIFTS), 0) == iota((SHIFTS, SHIFTS), 1)
    step_x = unit * jnp.sum(jnp.where(eye12, shifts[0:1, :], 0.0), axis=1, keepdims=True)
    step_y = unit * jnp.sum(jnp.where(eye12, shifts[1:2, :], 0.0), axis=1, keepdims=True)

    def tables(step):
        lane12 = iota((SHIFTS, 128), 1)
        base = step_x * (lane12 % 64).astype(F32) + step_y * (lane12 // 64).astype(F32)
        tile = step_y * (2 * lane12 - 64).astype(F32)
        base_c, base_s, tile_c, tile_s = jnp.cos(base), jnp.sin(base), jnp.cos(tile), jnp.sin(tile)
        for t in range(64):
            half, col = t // 32, (t % 32) * 128
            tc, ts = tile_c[:, t : t + 1], tile_s[:, t : t + 1]
            cos_t[half, :, col : col + 128] = base_c * tc - base_s * ts
            sin_t[half, :, col : col + 128] = base_s * tc + base_c * ts

    def rotate(step):
        if step == 0:
            loads[2].wait()
        col = step * 256
        for half in range(2):
            real = refs[:, half * QUART + col : half * QUART + col + 256].astype(F32)
            imag = refs[:, (2 + half) * QUART + col : (2 + half) * QUART + col + 256].astype(F32)
            for s in range(SHIFTS):
                cs, sn = cos_t[half, s : s + 1, col : col + 256], sin_t[half, s : s + 1, col : col + 256]
                r = row(half, s, 0)
                rot[r : r + 16, col : col + 256] = (real * cs - imag * sn).astype(BF16)
                rot[r + 16 : r + 32, col : col + 256] = (real * sn + imag * cs).astype(BF16)

    def routing(step):
        loads[3].wait()
        loads[4].wait()
        eye = iota((128, 128), 0) == iota((128, 128), 1)
        row_col = jnp.sum(jnp.where(eye, slot_rows[...].astype(F32), 0.0), axis=1, keepdims=True)
        own_col = jnp.sum(jnp.where(eye, owners[...].astype(F32), 0.0), axis=1, keepdims=True)
        blocks = [(q * 32 + u * 8) for u in range(4) for q in range(4)]
        row_col = jnp.concatenate([row_col[b : b + 8] for b in blocks], axis=0)
        own_col = jnp.concatenate([own_col[b : b + 8] for b in blocks], axis=0)
        lane128 = iota((128, 128), 1).astype(F32)
        owner_hot = (own_col == lane128).astype(F32)
        before = (iota((128, 128), 1) < iota((128, 128), 0)).astype(BF16)
        counts = jnp.dot(before, owner_hot.astype(BF16), preferred_element_type=F32)
        rank_col = jnp.sum(counts * owner_hot, axis=1, keepdims=True)
        slot_col = own_col * CAP + rank_col
        slot_row = jnp.sum(jnp.where(eye, slot_col, 0.0), axis=0, keepdims=True)
        oh[...] = (slot_row == iota((SLOTS, 128), 0).astype(F32)).astype(BF16)
        oh_t[...] = (slot_col == iota((128, SLOTS), 1).astype(F32)).astype(BF16)
        rank_rows = jnp.where(rank_col == lane128, row_col + 1.0, 0.0).astype(BF16)
        table = lax.dot_general(
            owner_hot.astype(BF16), rank_rows, (((0,), (0,)), ((), ())), preferred_element_type=F32
        ) - 1.0
        for d in range(N_ORI):
            meta_s[d] = table[d : d + 1, :]

    def pass_token(step):
        if step:
            for way in range(2):
                pl.semaphore_wait(token.at[step - 1, way], 1)
        if step < 4:
            for way, to in enumerate((up, down)):
                pl.semaphore_signal(token.at[step, way], 1, device_id={"img": to}, device_id_type=MESH)

    pl.semaphore_wait(barrier, len(near) + 3)

    def gather_copy(block, dx, dy, to):
        src = lax.rem(x + NX - dx, NX) * NY + lax.rem(y + NY - dy, NY)
        ref = gat.at[src, :, pl.ds(block[1], block[2] - block[1])]
        return pltpu.make_async_remote_copy(
            src_ref=ref, dst_ref=ref, send_sem=gat_send, recv_sem=gat_recv.at[number[block]],
            device_id={"ori": to}, device_id_type=MESH,
        )

    xs = [lax.rem(x + d, NX) * NY for d in range(NX)]
    ys = [lax.rem(y + d, NY) for d in range(NY)]
    others = sorted(
        ((a, b) for a in range(NX) for b in range(NY) if a or b), key=lambda p: -min(p[0], NX - p[0]) - min(p[1], NY - p[1])
    )

    def spread(send_ref, recv_ref, which):
        for a, b in others:
            to = xs[a] + ys[b]
            src = send_ref.at[0] if send_ref.shape[0] == 1 else send_ref.at[to]
            pltpu.make_async_remote_copy(
                src_ref=src, dst_ref=recv_ref.at[me_o], send_sem=sends.at[which], recv_sem=recvs.at[which],
                device_id={"ori": to}, device_id_type=MESH,
            ).start()

    def await_bytes(ref, sem):
        pltpu.make_async_copy(ref, ref, sem).wait()

    jobs = [(pass_token, 0), (tables, 0)]
    jobs += [(rotate, i) for i in range(QUART // 256)]
    jobs[6:6] = [(pass_token, 1)]
    jobs[10:10] = [(pass_token, 2)]
    jobs[14:14] = [(pass_token, 3)]
    jobs += [(pass_token, 4), (routing, 0)]
    due = [1] * 8 + [5 + i * (len(plan) - 12) // (len(jobs) - 8) for i in range(len(jobs) - 8)]
    for i, (block, hops) in enumerate(plan):
        dx, dy = block[3:5]
        if dx or dy:
            gather_copy(block, dx, dy, me_o).wait_recv()
        for axis, dist, to in hops:
            gather_copy(to, dx, dy, along(axis, dist)).start()
        while due and due[0] <= i:
            due.pop(0)
            job, step = jobs.pop(0)
            job(step)
    for job, step in jobs:
        job(step)
    for h in range(2):
        acc[h * 384 : h * 384 + 384, :] = lax.dot_general(
            rot[h * 384 : h * 384 + 384, :], gat[...].reshape(N_ORI * 8, QUART), (((1,), (1,)), ((), ())),
            preferred_element_type=F32)

    quarter = iota((16, 256), 1) % 8 // 2
    places = [(half, im) for half in range(2) for im in range(2)]
    mine = []
    for s in range(SHIFTS):
        mine.append(
            sum(
                jnp.where(quarter == 2 * im + half, acc[row(half, s, im) : row(half, s, im) + 16, :], 0.0)
                for half, im in places
            )
        )
    mine = jnp.concatenate(mine, axis=0)
    left, right = iota((256, 256), 0), iota((256, 256), 1)
    fold = ((left // 8 == right // 8) & (left % 2 == right % 2)).astype(F32)
    scores = jnp.dot(mine, fold, precision=HIGH, preferred_element_type=F32) * (2.0 / math.sqrt(COEF))
    peak = jnp.max(scores, axis=0, keepdims=True)
    expo = jnp.exp(scores - peak)
    total = jnp.sum(expo, axis=0, keepdims=True)
    stat = jnp.where(iota((1, 256), 1) // 2 % 2 == 0, peak, total)
    stat_s[0] = stat
    spread(stat_s, stat_r, 1)
    stat_r[me_o] = stat
    spread(meta_s, meta_r, 0)
    meta_r[me_o] = meta_s[me_o]
    loads[5].wait()
    loads[6].wait()

    await_bytes(stat_r.at[pl.ds(0, N_ORI - 1)], recvs.at[1])
    stats = stat_r[...].reshape(N_ORI, 256)
    even = iota((N_ORI, 256), 1) // 2 % 2 == 0
    peaks = jnp.where(even, stats, pltpu.roll(stats, 2, 1))
    totals = jnp.where(even, pltpu.roll(stats, 254, 1), stats)
    top = jnp.max(peaks, axis=0, keepdims=True)
    whole = jnp.sum(totals * jnp.exp(peaks - top), axis=0, keepdims=True)
    weights = expo * (jnp.exp(peak - top) / whole)
    for s in range(SHIFTS):
        for half, im in places:
            r = row(half, s, im)
            wts[r : r + 16, :] = jnp.where(quarter == 2 * im + half, weights[s * 16 : s * 16 + 16], 0.0).astype(BF16)

    def pair_copy(u):
        return pltpu.make_async_remote_copy(
            src_ref=pair_s.at[u], dst_ref=pair_r.at[u], send_sem=pair_send.at[u], recv_sem=pair_recv.at[u],
            device_id={"img": z * 2 + 1 - c}, device_id_type=MESH,
        )

    def project(u):
        for half in range(2):
            res, ims = [], []
            for v in range(1024 // 512):
                cols = slice(u * 1024 + v * 512, u * 1024 + v * 512 + 512)
                block = gat[:, :, cols].reshape(N_ORI * 8, 512)
                prod = jnp.dot(wts[half * 384 : half * 384 + 384, :], block, preferred_element_type=F32)
                re = jnp.zeros((16, 512), F32)
                im = jnp.zeros((16, 512), F32)
                for s in range(SHIFTS):
                    cs, sn = cos_t[half, s : s + 1, cols], sin_t[half, s : s + 1, cols]
                    sr = prod[s * 32 : s * 32 + 16, :]
                    si = prod[s * 32 + 16 : s * 32 + 32, :]
                    re = re + sr * cs + si * sn
                    im = im - sr * sn + si * cs
                res.append(re)
                ims.append(im)
            for first, sums in ((half * 8, res), (16 + half * 8, ims)):
                part[u, :, first : first + 8, :] = jnp.concatenate(sums, axis=1).reshape(16, 8, 128)
        for k in range(NZ):
            pair_s[u, k] = part[u, 2 * k + 1 - c].astype(BF16)
        pair_copy(u).start()

    zs = [lax.rem(z + d, NZ) for d in range(NZ)]

    def chip_sum(u, to):
        return part[u, 2 * to + c] + pair_r[u, to].astype(F32)

    def z_copy(u, src, dst, dist, sem):
        return pltpu.make_async_remote_copy(
            src_ref=src, dst_ref=dst, send_sem=z_send.at[u], recv_sem=sem,
            device_id={"img": zs[dist % NZ] * 2 + c}, device_id_type=MESH,
        )

    def first_leg(u):
        pair_copy(u).wait_recv()
        own_tot[u] = chip_sum(u, z)
        if u == 3:
            for d in (4, 3, 5, 2, 6, 1, 7):
                z_s[u, d] = chip_sum(u, zs[d]).astype(BF16)
                z_copy(u, z_s.at[u, d], z_r.at[u, NZ - d], d, z_recv.at[u, 0]).start()
            return
        z_s[u, 4] = chip_sum(u, zs[4]).astype(BF16)
        for way, (far, via, near_by) in enumerate(((3, 1, 1), (5, 7, 7))):
            z_s[u, far] = chip_sum(u, zs[far]).astype(BF16)
            half = pl.ds(way * 16, 16)
            z_copy(u, z_s.at[u, 4, half], relay_r.at[u, 2 + way, half], 2 * via, z_recv.at[u, 3 + way]).start()
            z_copy(u, z_s.at[u, far], relay_r.at[u, way], via, z_recv.at[u, 1 + way]).start()
            z_s[u, near_by] = chip_sum(u, zs[near_by]).astype(BF16)
        for near_by in (1, 7):
            z_copy(u, z_s.at[u, near_by], z_r.at[u, NZ - near_by], near_by, z_recv.at[u, 0]).start()

    def second_leg(u):
        for way, (to, other) in enumerate(((2, 16), (6, 0))):
            await_bytes(relay_r.at[u, way], z_recv.at[u, 1 + way])
            half = pl.ds(way * 16, 16)
            await_bytes(relay_r.at[u, 2 + way, half], z_recv.at[u, 3 + way])
            total = chip_sum(u, zs[to]) + relay_r[u, way].astype(F32)
            far = relay_r[u, 2 + way, way * 16 : way * 16 + 16, :].astype(F32)
            zero = jnp.zeros((16, 128), F32)
            total = total + jnp.concatenate([zero, far] if way else [far, zero], axis=0)
            z_s[u, to] = total.astype(BF16)
            z_copy(u, z_s.at[u, to], z_r.at[u, NZ - to], to, z_recv.at[u, 0]).start()

    project(0)

    mass16 = weights[0:16]
    for s in range(1, SHIFTS):
        mass16 = mass16 + weights[s * 16 : s * 16 + 16]
    mass16 = jnp.sum(jnp.where(quarter == 0, mass16, 0.0), axis=1, keepdims=True)
    mass16 = jnp.broadcast_to(mass16, (16, 128))
    for o in range(N_IMG):
        mz_s[o] = mass16[o : o + 1, :]

    def send_mass(p, carry):
        to = lax.rem(me_i + p, N_IMG)
        pltpu.make_async_remote_copy(
            src_ref=mz_s.at[to], dst_ref=mz_r.at[me_i], send_sem=sends.at[2], recv_sem=recvs.at[2],
            device_id={"img": to}, device_id_type=MESH,
        ).start()
        return carry

    lax.fori_loop(1, N_IMG, send_mass, 0)
    mz_r[me_i] = mz_s[me_i]

    for u in range(1, 4):
        project(u)
        first_leg(u - 1)
    first_leg(3)
    for u in range(3):
        second_leg(u)

    await_bytes(mz_r.at[pl.ds(0, N_IMG - 1)], recvs.at[2])
    mass_all = jnp.sum(mz_r[...].reshape(N_IMG, 128), axis=0, keepdims=True)
    mb_s[0] = mass_all
    spread(mb_s, mb_r, 3)
    mb_r[me_o] = mass_all

    await_bytes(meta_r.at[pl.ds(0, N_ORI - 1)], recvs.at[0])
    rep = (iota((SLOTS, N_ORI), 0) // CAP == iota((SLOTS, N_ORI), 1)).astype(BF16)
    rid = jnp.dot(rep, meta_r[...].reshape(N_ORI, 128).astype(BF16), preferred_element_type=F32)
    rid = jnp.where(iota((SLOTS, 128), 0) % CAP == iota((SLOTS, 128), 1), rid, 0.0)
    hot = (jnp.sum(rid, axis=1, keepdims=True) == iota((SLOTS, 128), 1).astype(F32)).astype(F32)
    scat_t[...] = hot.astype(BF16)
    scat[...] = jnp.transpose(hot).astype(BF16)
    cnt[...] = jnp.dot(scat[...], rep, preferred_element_type=F32)
    reg_col = jnp.sum(
        jnp.where(iota((ROWS, ROWS), 0) == iota((ROWS, ROWS), 1), reg[...], 0.0), axis=1, keepdims=True
    )

    gram = lax.dot_general(
        interp[...], interp[...], (((1,), (1,)), ((), ())), precision=HIGH, preferred_element_type=F32
    )

    sums = []
    for u in range(4):
        sources = (1, 2, 6, 7) if u < 3 else range(1, NZ)
        await_bytes(z_r.at[u, pl.ds(0, len(sources))], z_recv.at[u, 0])
        tot = own_tot[u]
        for d in sources:
            tot = tot + z_r[u, d].astype(F32)
        sums.append(tot)
    segments = jnp.concatenate(sums, axis=0).astype(BF16)

    val_s[...] = jnp.dot(oh[...], segments, preferred_element_type=F32).astype(BF16).reshape(N_ORI, CAP, 128)
    spread(val_s, val_r, 4)
    val_r[me_o] = val_s[me_o]

    await_bytes(mb_r.at[pl.ds(0, N_ORI - 1)], recvs.at[3])
    weight_sum = jnp.dot(
        cnt[0:ROWS, :], mb_r[...].reshape(N_ORI, 128), precision=HIGH, preferred_element_type=F32
    )
    inverse = 1.0 / (weight_sum + reg_col)

    await_bytes(val_r.at[pl.ds(0, N_ORI - 1)], recvs.at[4])
    inserted = jnp.dot(scat[0:ROWS, :], val_r[...].reshape(SLOTS, 128), preferred_element_type=F32)
    back = jnp.dot(inserted, gram, precision=HIGH, preferred_element_type=F32) * inverse
    reply = jnp.dot(scat_t[:, 0:ROWS], back.astype(BF16), preferred_element_type=F32)
    rep_s[...] = reply.astype(BF16).reshape(N_ORI, CAP, 128)
    spread(rep_s, rep_r, 5)
    rep_r[me_o] = rep_s[me_o]
    out[0:ROWS, :] = jnp.dot(inserted, interp[...], precision=HIGH, preferred_element_type=F32) * inverse

    await_bytes(gat.at[pl.ds(0, N_ORI - 1)], gat_send)
    for u in range(4):
        pair_copy(u).wait_send()
        await_bytes(z_s.at[u, pl.ds(0, NZ - 1)], z_send.at[u])
    await_bytes(meta_s.at[pl.ds(0, N_ORI - 1)], sends.at[0])
    await_bytes(stat_r.at[pl.ds(0, N_ORI - 1)], sends.at[1])
    await_bytes(mz_s.at[pl.ds(0, N_IMG - 1)], sends.at[2])
    await_bytes(mb_r.at[pl.ds(0, N_ORI - 1)], sends.at[3])
    await_bytes(val_s.at[pl.ds(0, N_ORI - 1)], sends.at[4])

    await_bytes(rep_r.at[pl.ds(0, N_ORI - 1)], recvs.at[5])
    picked = jnp.dot(oh_t[...], rep_r[...].reshape(SLOTS, 128), preferred_element_type=F32)
    for u in range(4):
        for q in range(4):
            to = ROWS + q * 32 + u * 8
            out[to : to + 8, :] = picked[u * 32 + q * 8 : u * 32 + q * 8 + 8, :]
    await_bytes(rep_s.at[pl.ds(0, N_ORI - 1)], sends.at[5])


def hand_over(both, vol, res):
    vol[...] = both[0:ROWS, :]
    res[...] = both[ROWS : ROWS + 128, :]


def shards(images, references, shifts, owners, slot_rows, interpolation, regularizer):
    vmem = pl.BlockSpec(memory_space=pltpu.VMEM)
    anywhere = pl.BlockSpec(memory_space=pl.ANY)
    operands = (
        images,
        references,
        shifts.T,
        owners.reshape(1, 128),
        slot_rows.reshape(1, 128),
        interpolation,
        regularizer.reshape(1, ROWS),
    )
    both = pl.pallas_call(
        kernel,
        out_shape=jax.ShapeDtypeStruct((ROWS + 128, 128), F32),
        in_specs=[anywhere] * 7,
        out_specs=vmem,
        scratch_shapes=[
            pltpu.VMEM((2, COEF), BF16),
            pltpu.VMEM((16, COEF), BF16),
            pltpu.VMEM((2, SHIFTS), F32),
            pltpu.VMEM((1, 128), jnp.int32),
            pltpu.VMEM((1, 128), jnp.int32),
            pltpu.VMEM((128, 128), F32),
            pltpu.VMEM((1, ROWS), F32),
            pltpu.VMEM((N_ORI, 8, QUART), BF16),
            pltpu.VMEM((768, QUART), BF16),
            pltpu.VMEM((2, SHIFTS, QUART), F32),
            pltpu.VMEM((2, SHIFTS, QUART), F32),
            pltpu.VMEM((768, 256), F32),
            pltpu.VMEM((768, 256), BF16),
            pltpu.VMEM((4, N_IMG, 32, 128), F32),
            pltpu.VMEM((4, 32, 128), F32),
            pltpu.VMEM((4, NZ, 32, 128), BF16),
            pltpu.VMEM((4, NZ, 32, 128), BF16),
            pltpu.VMEM((4, NZ, 32, 128), BF16),
            pltpu.VMEM((4, NZ, 32, 128), BF16),
            pltpu.VMEM((3, 4, 32, 128), BF16),
            pltpu.VMEM((N_ORI, 1, 128), F32),
            pltpu.VMEM((N_ORI, 1, 128), F32),
            pltpu.VMEM((1, 1, 256), F32),
            pltpu.VMEM((N_ORI, 1, 256), F32),
            pltpu.VMEM((N_IMG, 1, 128), F32),
            pltpu.VMEM((N_IMG, 1, 128), F32),
            pltpu.VMEM((1, 1, 128), F32),
            pltpu.VMEM((N_ORI, 1, 128), F32),
            pltpu.VMEM((N_ORI, CAP, 128), BF16),
            pltpu.VMEM((N_ORI, CAP, 128), BF16),
            pltpu.VMEM((N_ORI, CAP, 128), BF16),
            pltpu.VMEM((N_ORI, CAP, 128), BF16),
            pltpu.VMEM((SLOTS, 128), BF16),
            pltpu.VMEM((128, SLOTS), BF16),
            pltpu.VMEM((128, SLOTS), BF16),
            pltpu.VMEM((SLOTS, 128), BF16),
            pltpu.VMEM((128, N_ORI), F32),
            pltpu.SemaphoreType.DMA((7,)),
            pltpu.SemaphoreType.DMA,
            pltpu.SemaphoreType.DMA((len(gather_plan()),)),
            pltpu.SemaphoreType.DMA((4,)),
            pltpu.SemaphoreType.DMA((4,)),
            pltpu.SemaphoreType.DMA((4,)),
            pltpu.SemaphoreType.DMA((4, 5)),
            pltpu.SemaphoreType.DMA((6,)),
            pltpu.SemaphoreType.DMA((6,)),
            pltpu.SemaphoreType.REGULAR((4, 2)),
        ],
        compiler_params=pltpu.CompilerParams(
            collective_id=0, has_side_effects=True, vmem_limit_bytes=40 * 1024 * 1024
        ),
    )(*(pltpu.with_memory_space_constraint(operand, pltpu.HBM) for operand in operands))
    volume, resampled = pl.pallas_call(
        hand_over,
        out_shape=(jax.ShapeDtypeStruct((ROWS, 128), F32), jax.ShapeDtypeStruct((128, 128), F32)),
        in_specs=[vmem],
        out_specs=(vmem, vmem),
        compiler_params=pltpu.CompilerParams(vmem_limit_bytes=4 * 1024 * 1024),
    )(both)
    return (volume, resampled.reshape(1, COEF))


def solution(mesh):
    in_specs = (
        P(("img", "ori"), None),
        P("ori", None),
        P(),
        P(("ori", "img"), None),
        P(("ori", "img")),
        P(("ori", "img"), None),
        P(("ori", "img")),
    )
    out_specs = (P(("ori", "img"), None), P(("ori", "img"), None))
    return jax.shard_map(shards, mesh=mesh, in_specs=in_specs, out_specs=out_specs, check_vma=False)
```

```python
import heapq
import math

import jax
import jax.numpy as jnp
from jax import lax
from jax.experimental import pallas as pl
from jax.experimental.pallas import tpu as pltpu
from jax.sharding import PartitionSpec as P

NX, NY, NZ = 4, 8, 8
N_ORI = NX * NY
N_IMG = 2 * NZ
COEF = 16384
QUART = COEF // 4
SHIFTS = 12
CAP = 16
SLOTS = N_ORI * CAP
ROWS = 64
MESH = pl.DeviceIdType.MESH
SCORE_COLS = 2048
HIGH = lax.Precision.HIGHEST
F32, BF16 = jnp.float32, jnp.bfloat16

SPLIT = 1536
RANGE = {"A": (0, SPLIT), "B": (SPLIT, QUART)}
PARENT = {"A": ((0, 0, 1), (0, 0, 1, 2, 2)), "B": ((0, 0, 1), (0, 0, 0, 2, 2))}


def ring_steps(parents, size, d, sign, lo, hi, mid):
    for k in range(1, size // 2 + 1):
        for way in (1, -1):
            if d != way * parents[k] % size or d and sign != way:
                continue
            a, b = lo, hi
            if k == size // 2:
                a, b = (lo, min(hi, mid)) if way > 0 else (max(lo, mid), hi)
            if a < b:
                yield way, way * k % size, k - parents[k], a, b


def forwards(block):
    route, lo, hi, dx, dy, sx, sy = block
    mid = sum(RANGE[route]) // 2
    par_x, par_y = PARENT[route]
    out = []
    if route == "A" or dx == 0:
        for way, d, hops, a, b in ring_steps(par_y, NY, dy, sy, lo, hi, mid):
            out.append(("y", way * hops, (route, a, b, dx, d, sx, way)))
    if route == "B" or dy == 0:
        for way, d, hops, a, b in ring_steps(par_x, NX, dx, sx, lo, hi, mid):
            out.append(("x", way * hops, (route, a, b, d, dy, way, sy)))
    return out


def depth(block):
    return max((1.4 + 0.7 * abs(h) + depth(k) for _, h, k in forwards(block)), default=0)


def gather_plan():
    heap = [(0.0, i, (r, *RANGE[r], 0, 0, 0, 0)) for i, r in enumerate("BA")]
    free, plan, count = {}, [], 10
    while heap:
        when, _, block = heapq.heappop(heap)
        hops = sorted(forwards(block), key=lambda f: -depth(f[2]) - 0.7 * abs(f[1]))
        plan.append((block, hops))
        for axis, dist, to in hops:
            wire = axis, dist > 0
            took = (to[2] - to[1]) * 16 / 46.5e3 + 0.03
            begin = max(when, free.get(wire, 0.0))
            free[wire] = begin + took * abs(dist)
            count += 1
            heapq.heappush(heap, (begin + took + 1.4 + 0.7 * abs(dist), count, to))
    return plan


def row(half, s, part):
    return ((half * SHIFTS + s) * 2 + part) * 16


def iota(shape, dim):
    return lax.broadcasted_iota(jnp.int32, shape, dim)


def kernel(
    images_h, refs_h, shifts_h, owners_h, rows_h, interp_h, reg_h,
    out,
    images, refs, shifts, owners, slot_rows, interp, reg,
    gat, rot, cos_t, sin_t, acc, wts, part, own_tot, pair_s, pair_r, z_s, z_r, relay_r,
    meta_s, meta_r, stat_s, stat_r, mz_s, mz_r, mb_s, mb_r, val_s, val_r, rep_s, rep_r,
    oh, oh_t, scat, scat_t, cnt,
    loc_sem, gat_send, gat_recv, pair_send, pair_recv, z_send, z_recv, sends, recvs, token,
):
    me_i, me_o = lax.axis_index("img"), lax.axis_index("ori")
    x, y = me_o // NY, lax.rem(me_o, NY)
    z, c = me_i // 2, lax.rem(me_i, 2)
    up, down = lax.rem(z + 1, NZ) * 2 + c, lax.rem(z + NZ - 1, NZ) * 2 + c

    def along(axis, dist):
        if axis == "x":
            return lax.rem(x + NX + dist, NX) * NY + y
        return x * NY + lax.rem(y + NY + dist, NY)

    plan = gather_plan()
    number = {block: i for i, (block, _) in enumerate(plan)}
    near = sorted({(axis, dist) for _, hops in plan for axis, dist, _ in hops})
    barrier = pltpu.get_barrier_semaphore()
    for axis, dist in near:
        pl.semaphore_signal(barrier, 1, device_id={"ori": along(axis, dist)}, device_id_type=MESH)
    for to in (up, down, z * 2 + 1 - c):
        pl.semaphore_signal(barrier, 1, device_id={"img": to}, device_id_type=MESH)

    loads = [
        pltpu.make_async_copy(src, dst, loc_sem.at[i])
        for i, (src, dst) in enumerate(
            [(images_h, images), (shifts_h, shifts), (refs_h, refs), (owners_h, owners), (rows_h, slot_rows),
             (interp_h, interp), (reg_h, reg)]
        )
    ]
    for copy in loads:
        copy.start()

    loads[0].wait()
    gat[me_o] = jnp.concatenate(
        [images[:, q * QUART : (q + 1) * QUART].astype(F32) for q in range(4)], axis=0
    ).astype(BF16)
    loads[1].wait()

    unit = 2.0 * math.pi / 128.0
    eye12 = iota((SHIFTS, SHIFTS), 0) == iota((SHIFTS, SHIFTS), 1)
    step_x = unit * jnp.sum(jnp.where(eye12, shifts[0:1, :], 0.0), axis=1, keepdims=True)
    step_y = unit * jnp.sum(jnp.where(eye12, shifts[1:2, :], 0.0), axis=1, keepdims=True)

    def tables(step):
        lane12 = iota((SHIFTS, 128), 1)
        base = step_x * (lane12 % 64).astype(F32) + step_y * (lane12 // 64).astype(F32)
        tile = step_y * (2 * lane12 - 64).astype(F32)
        base_c, base_s, tile_c, tile_s = jnp.cos(base), jnp.sin(base), jnp.cos(tile), jnp.sin(tile)
        for t in range(64):
            half, col = t // 32, (t % 32) * 128
            tc, ts = tile_c[:, t : t + 1], tile_s[:, t : t + 1]
            cos_t[half, :, col : col + 128] = base_c * tc - base_s * ts
            sin_t[half, :, col : col + 128] = base_s * tc + base_c * ts

    def rotate(step):
        if step == 0:
            loads[2].wait()
        col = step * 256
        for half in range(2):
            real = refs[:, half * QUART + col : half * QUART + col + 256].astype(F32)
            imag = refs[:, (2 + half) * QUART + col : (2 + half) * QUART + col + 256].astype(F32)
            for s in range(SHIFTS):
                cs, sn = cos_t[half, s : s + 1, col : col + 256], sin_t[half, s : s + 1, col : col + 256]
                r = row(half, s, 0)
                rot[r : r + 16, col : col + 256] = (real * cs - imag * sn).astype(BF16)
                rot[r + 16 : r + 32, col : col + 256] = (real * sn + imag * cs).astype(BF16)

    def routing(step):
        loads[3].wait()
        loads[4].wait()
        eye = iota((128, 128), 0) == iota((128, 128), 1)
        row_col = jnp.sum(jnp.where(eye, slot_rows[...].astype(F32), 0.0), axis=1, keepdims=True)
        own_col = jnp.sum(jnp.where(eye, owners[...].astype(F32), 0.0), axis=1, keepdims=True)
        blocks = [(q * 32 + u * 8) for u in range(4) for q in range(4)]
        row_col = jnp.concatenate([row_col[b : b + 8] for b in blocks], axis=0)
        own_col = jnp.concatenate([own_col[b : b + 8] for b in blocks], axis=0)
        lane128 = iota((128, 128), 1).astype(F32)
        owner_hot = (own_col == lane128).astype(F32)
        before = (iota((128, 128), 1) < iota((128, 128), 0)).astype(BF16)
        counts = jnp.dot(before, owner_hot.astype(BF16), preferred_element_type=F32)
        rank_col = jnp.sum(counts * owner_hot, axis=1, keepdims=True)
        slot_col = own_col * CAP + rank_col
        slot_row = jnp.sum(jnp.where(eye, slot_col, 0.0), axis=0, keepdims=True)
        oh[...] = (slot_row == iota((SLOTS, 128), 0).astype(F32)).astype(BF16)
        oh_t[...] = (slot_col == iota((128, SLOTS), 1).astype(F32)).astype(BF16)
        rank_rows = jnp.where(rank_col == lane128, row_col + 1.0, 0.0).astype(BF16)
        table = lax.dot_general(
            owner_hot.astype(BF16), rank_rows, (((0,), (0,)), ((), ())), preferred_element_type=F32
        ) - 1.0
        for d in range(N_ORI):
            meta_s[d] = table[d : d + 1, :]

    def pass_token(step):
        if step:
            for way in range(2):
                pl.semaphore_wait(token.at[step - 1, way], 1)
        if step < 4:
            for way, to in enumerate((up, down)):
                pl.semaphore_signal(token.at[step, way], 1, device_id={"img": to}, device_id_type=MESH)

    pl.semaphore_wait(barrier, len(near) + 3)

    def gather_copy(block, dx, dy, to):
        src = lax.rem(x + NX - dx, NX) * NY + lax.rem(y + NY - dy, NY)
        ref = gat.at[src, :, pl.ds(block[1], block[2] - block[1])]
        return pltpu.make_async_remote_copy(
            src_ref=ref, dst_ref=ref, send_sem=gat_send, recv_sem=gat_recv.at[number[block]],
            device_id={"ori": to}, device_id_type=MESH,
        )

    xs = [lax.rem(x + d, NX) * NY for d in range(NX)]
    ys = [lax.rem(y + d, NY) for d in range(NY)]
    others = sorted(
        ((a, b) for a in range(NX) for b in range(NY) if a or b), key=lambda p: -min(p[0], NX - p[0]) - min(p[1], NY - p[1])
    )

    def spread(send_ref, recv_ref, which):
        for a, b in others:
            to = xs[a] + ys[b]
            src = send_ref.at[0] if send_ref.shape[0] == 1 else send_ref.at[to]
            pltpu.make_async_remote_copy(
                src_ref=src, dst_ref=recv_ref.at[me_o], send_sem=sends.at[which], recv_sem=recvs.at[which],
                device_id={"ori": to}, device_id_type=MESH,
            ).start()

    def await_bytes(ref, sem):
        pltpu.make_async_copy(ref, ref, sem).wait()

    jobs = [(pass_token, 0), (tables, 0)]
    jobs += [(rotate, i) for i in range(QUART // 256)]
    jobs[6:6] = [(pass_token, 1)]
    jobs[10:10] = [(pass_token, 2)]
    jobs[14:14] = [(pass_token, 3)]
    jobs += [(pass_token, 4), (routing, 0)]
    due = [1] * 8 + [5 + i * (len(plan) - 12) // (len(jobs) - 8) for i in range(len(jobs) - 8)]
    for i, (block, hops) in enumerate(plan):
        dx, dy = block[3:5]
        if dx or dy:
            gather_copy(block, dx, dy, me_o).wait_recv()
        for axis, dist, to in hops:
            gather_copy(to, dx, dy, along(axis, dist)).start()
        while due and due[0] <= i:
            due.pop(0)
            job, step = jobs.pop(0)
            job(step)
    for job, step in jobs:
        job(step)
    for h in range(2):
        acc[h * 384 : h * 384 + 384, :] = lax.dot_general(
            rot[h * 384 : h * 384 + 384, :], gat[...].reshape(N_ORI * 8, QUART), (((1,), (1,)), ((), ())),
            preferred_element_type=F32)

    quarter = iota((16, 256), 1) % 8 // 2
    places = [(half, im) for half in range(2) for im in range(2)]
    mine = []
    for s in range(SHIFTS):
        mine.append(
            sum(
                jnp.where(quarter == 2 * im + half, acc[row(half, s, im) : row(half, s, im) + 16, :], 0.0)
                for half, im in places
            )
        )
    mine = jnp.concatenate(mine, axis=0)
    left, right = iota((256, 256), 0), iota((256, 256), 1)
    fold = ((left // 8 == right // 8) & (left % 2 == right % 2)).astype(F32)
    scores = jnp.dot(mine, fold, precision=HIGH, preferred_element_type=F32) * (2.0 / math.sqrt(COEF))
    peak = jnp.max(scores, axis=0, keepdims=True)
    expo = jnp.exp(scores - peak)
    total = jnp.sum(expo, axis=0, keepdims=True)
    stat = jnp.where(iota((1, 256), 1) // 2 % 2 == 0, peak, total)
    stat_s[0] = stat
    spread(stat_s, stat_r, 1)
    stat_r[me_o] = stat
    spread(meta_s, meta_r, 0)
    meta_r[me_o] = meta_s[me_o]
    loads[5].wait()
    loads[6].wait()

    await_bytes(stat_r.at[pl.ds(0, N_ORI - 1)], recvs.at[1])
    stats = stat_r[...].reshape(N_ORI, 256)
    even = iota((N_ORI, 256), 1) // 2 % 2 == 0
    peaks = jnp.where(even, stats, pltpu.roll(stats, 2, 1))
    totals = jnp.where(even, pltpu.roll(stats, 254, 1), stats)
    top = jnp.max(peaks, axis=0, keepdims=True)
    whole = jnp.sum(totals * jnp.exp(peaks - top), axis=0, keepdims=True)
    weights = expo * (jnp.exp(peak - top) / whole)
    for s in range(SHIFTS):
        for half, im in places:
            r = row(half, s, im)
            wts[r : r + 16, :] = jnp.where(quarter == 2 * im + half, weights[s * 16 : s * 16 + 16], 0.0).astype(BF16)

    def pair_copy(u):
        return pltpu.make_async_remote_copy(
            src_ref=pair_s.at[u], dst_ref=pair_r.at[u], send_sem=pair_send.at[u], recv_sem=pair_recv.at[u],
            device_id={"img": z * 2 + 1 - c}, device_id_type=MESH,
        )

    def project(u):
        for half in range(2):
            res, ims = [], []
            for v in range(1024 // 512):
                cols = slice(u * 1024 + v * 512, u * 1024 + v * 512 + 512)
                block = gat[:, :, cols].reshape(N_ORI * 8, 512)
                prod = jnp.dot(wts[half * 384 : half * 384 + 384, :], block, preferred_element_type=F32)
                re = jnp.zeros((16, 512), F32)
                im = jnp.zeros((16, 512), F32)
                for s in range(SHIFTS):
                    cs, sn = cos_t[half, s : s + 1, cols], sin_t[half, s : s + 1, cols]
                    sr = prod[s * 32 : s * 32 + 16, :]
                    si = prod[s * 32 + 16 : s * 32 + 32, :]
                    re = re + sr * cs + si * sn
                    im = im - sr * sn + si * cs
                res.append(re)
                ims.append(im)
            for first, sums in ((half * 8, res), (16 + half * 8, ims)):
                part[u, :, first : first + 8, :] = jnp.concatenate(sums, axis=1).reshape(16, 8, 128)
        for k in range(NZ):
            pair_s[u, k] = part[u, 2 * k + 1 - c].astype(BF16)
        pair_copy(u).start()

    zs = [lax.rem(z + d, NZ) for d in range(NZ)]

    def chip_sum(u, to):
        return part[u, 2 * to + c] + pair_r[u, to].astype(F32)

    def z_copy(u, src, dst, dist, sem):
        return pltpu.make_async_remote_copy(
            src_ref=src, dst_ref=dst, send_sem=z_send.at[u], recv_sem=sem,
            device_id={"img": zs[dist % NZ] * 2 + c}, device_id_type=MESH,
        )

    def first_leg(u):
        pair_copy(u).wait_recv()
        own_tot[u] = chip_sum(u, z)
        if u == 3:
            for d in (4, 3, 5, 2, 6, 1, 7):
                z_s[u, d] = chip_sum(u, zs[d]).astype(BF16)
                z_copy(u, z_s.at[u, d], z_r.at[u, NZ - d], d, z_recv.at[u, 0]).start()
            return
        z_s[u, 4] = chip_sum(u, zs[4]).astype(BF16)
        for way, (far, via, near_by) in enumerate(((3, 1, 1), (5, 7, 7))):
            z_s[u, far] = chip_sum(u, zs[far]).astype(BF16)
            half = pl.ds(way * 16, 16)
            z_copy(u, z_s.at[u, 4, half], relay_r.at[u, 2 + way, half], 2 * via, z_recv.at[u, 3 + way]).start()
            z_copy(u, z_s.at[u, far], relay_r.at[u, way], via, z_recv.at[u, 1 + way]).start()
            z_s[u, near_by] = chip_sum(u, zs[near_by]).astype(BF16)
        for near_by in (1, 7):
            z_copy(u, z_s.at[u, near_by], z_r.at[u, NZ - near_by], near_by, z_recv.at[u, 0]).start()

    def second_leg(u):
        for way, (to, other) in enumerate(((2, 16), (6, 0))):
            await_bytes(relay_r.at[u, way], z_recv.at[u, 1 + way])
            half = pl.ds(way * 16, 16)
            await_bytes(relay_r.at[u, 2 + way, half], z_recv.at[u, 3 + way])
            total = chip_sum(u, zs[to]) + relay_r[u, way].astype(F32)
            far = relay_r[u, 2 + way, way * 16 : way * 16 + 16, :].astype(F32)
            zero = jnp.zeros((16, 128), F32)
            total = total + jnp.concatenate([zero, far] if way else [far, zero], axis=0)
            z_s[u, to] = total.astype(BF16)
            z_copy(u, z_s.at[u, to], z_r.at[u, NZ - to], to, z_recv.at[u, 0]).start()

    project(0)
    project(1)
    project(2)
    first_leg(0)
    project(3)
    first_leg(1)
    first_leg(2)

    mass16 = weights[0:16]
    for s in range(1, SHIFTS):
        mass16 = mass16 + weights[s * 16 : s * 16 + 16]
    mass16 = jnp.sum(jnp.where(quarter == 0, mass16, 0.0), axis=1, keepdims=True)
    mass16 = jnp.broadcast_to(mass16, (16, 128))
    for o in range(N_IMG):
        mz_s[o] = mass16[o : o + 1, :]

    def send_mass(p, carry):
        to = lax.rem(me_i + p, N_IMG)
        pltpu.make_async_remote_copy(
            src_ref=mz_s.at[to], dst_ref=mz_r.at[me_i], send_sem=sends.at[2], recv_sem=recvs.at[2],
            device_id={"img": to}, device_id_type=MESH,
        ).start()
        return carry

    lax.fori_loop(1, N_IMG, send_mass, 0)
    mz_r[me_i] = mz_s[me_i]

    first_leg(3)
    for u in range(3):
        second_leg(u)

    await_bytes(mz_r.at[pl.ds(0, N_IMG - 1)], recvs.at[2])
    mass_all = jnp.sum(mz_r[...].reshape(N_IMG, 128), axis=0, keepdims=True)
    mb_s[0] = mass_all
    spread(mb_s, mb_r, 3)
    mb_r[me_o] = mass_all

    await_bytes(meta_r.at[pl.ds(0, N_ORI - 1)], recvs.at[0])
    rep = (iota((SLOTS, N_ORI), 0) // CAP == iota((SLOTS, N_ORI), 1)).astype(BF16)
    rid = jnp.dot(rep, meta_r[...].reshape(N_ORI, 128).astype(BF16), preferred_element_type=F32)
    rid = jnp.where(iota((SLOTS, 128), 0) % CAP == iota((SLOTS, 128), 1), rid, 0.0)
    hot = (jnp.sum(rid, axis=1, keepdims=True) == iota((SLOTS, 128), 1).astype(F32)).astype(F32)
    scat_t[...] = hot.astype(BF16)
    scat[...] = jnp.transpose(hot).astype(BF16)
    cnt[...] = jnp.dot(scat[...], rep, preferred_element_type=F32)
    reg_col = jnp.sum(
        jnp.where(iota((ROWS, ROWS), 0) == iota((ROWS, ROWS), 1), reg[...], 0.0), axis=1, keepdims=True
    )

    gram = lax.dot_general(
        interp[...], interp[...], (((1,), (1,)), ((), ())), precision=HIGH, preferred_element_type=F32
    )

    sums = []
    for u in range(4):
        sources = (1, 2, 6, 7) if u < 3 else range(1, NZ)
        await_bytes(z_r.at[u, pl.ds(0, len(sources))], z_recv.at[u, 0])
        tot = own_tot[u]
        for d in sources:
            tot = tot + z_r[u, d].astype(F32)
        sums.append(tot)
    segments = jnp.concatenate(sums, axis=0).astype(BF16)

    val_s[...] = jnp.dot(oh[...], segments, preferred_element_type=F32).astype(BF16).reshape(N_ORI, CAP, 128)
    spread(val_s, val_r, 4)
    val_r[me_o] = val_s[me_o]

    await_bytes(mb_r.at[pl.ds(0, N_ORI - 1)], recvs.at[3])
    weight_sum = jnp.dot(
        cnt[0:ROWS, :], mb_r[...].reshape(N_ORI, 128), precision=HIGH, preferred_element_type=F32
    )
    inverse = 1.0 / (weight_sum + reg_col)

    await_bytes(val_r.at[pl.ds(0, N_ORI - 1)], recvs.at[4])
    inserted = jnp.dot(scat[0:ROWS, :], val_r[...].reshape(SLOTS, 128), preferred_element_type=F32)
    back = jnp.dot(inserted, gram, precision=HIGH, preferred_element_type=F32) * inverse
    reply = jnp.dot(scat_t[:, 0:ROWS], back.astype(BF16), preferred_element_type=F32)
    rep_s[...] = reply.astype(BF16).reshape(N_ORI, CAP, 128)
    spread(rep_s, rep_r, 5)
    rep_r[me_o] = rep_s[me_o]
    out[0:ROWS, :] = jnp.dot(inserted, interp[...], precision=HIGH, preferred_element_type=F32) * inverse

    await_bytes(gat.at[pl.ds(0, N_ORI - 1)], gat_send)
    for u in range(4):
        pair_copy(u).wait_send()
        await_bytes(z_s.at[u, pl.ds(0, NZ - 1)], z_send.at[u])
    await_bytes(meta_s.at[pl.ds(0, N_ORI - 1)], sends.at[0])
    await_bytes(stat_r.at[pl.ds(0, N_ORI - 1)], sends.at[1])
    await_bytes(mz_s.at[pl.ds(0, N_IMG - 1)], sends.at[2])
    await_bytes(mb_r.at[pl.ds(0, N_ORI - 1)], sends.at[3])
    await_bytes(val_s.at[pl.ds(0, N_ORI - 1)], sends.at[4])

    await_bytes(rep_r.at[pl.ds(0, N_ORI - 1)], recvs.at[5])
    picked = jnp.dot(oh_t[...], rep_r[...].reshape(SLOTS, 128), preferred_element_type=F32)
    for u in range(4):
        for q in range(4):
            to = ROWS + q * 32 + u * 8
            out[to : to + 8, :] = picked[u * 32 + q * 8 : u * 32 + q * 8 + 8, :]
    await_bytes(rep_s.at[pl.ds(0, N_ORI - 1)], sends.at[5])


def hand_over(both, vol, res):
    vol[...] = both[0:ROWS, :]
    res[...] = both[ROWS : ROWS + 128, :]


def shards(images, references, shifts, owners, slot_rows, interpolation, regularizer):
    vmem = pl.BlockSpec(memory_space=pltpu.VMEM)
    anywhere = pl.BlockSpec(memory_space=pl.ANY)
    operands = (
        images,
        references,
        shifts.T,
        owners.reshape(1, 128),
        slot_rows.reshape(1, 128),
        interpolation,
        regularizer.reshape(1, ROWS),
    )
    both = pl.pallas_call(
        kernel,
        out_shape=jax.ShapeDtypeStruct((ROWS + 128, 128), F32),
        in_specs=[anywhere] * 7,
        out_specs=vmem,
        scratch_shapes=[
            pltpu.VMEM((2, COEF), BF16),
            pltpu.VMEM((16, COEF), BF16),
            pltpu.VMEM((2, SHIFTS), F32),
            pltpu.VMEM((1, 128), jnp.int32),
            pltpu.VMEM((1, 128), jnp.int32),
            pltpu.VMEM((128, 128), F32),
            pltpu.VMEM((1, ROWS), F32),
            pltpu.VMEM((N_ORI, 8, QUART), BF16),
            pltpu.VMEM((768, QUART), BF16),
            pltpu.VMEM((2, SHIFTS, QUART), F32),
            pltpu.VMEM((2, SHIFTS, QUART), F32),
            pltpu.VMEM((768, 256), F32),
            pltpu.VMEM((768, 256), BF16),
            pltpu.VMEM((4, N_IMG, 32, 128), F32),
            pltpu.VMEM((4, 32, 128), F32),
            pltpu.VMEM((4, NZ, 32, 128), BF16),
            pltpu.VMEM((4, NZ, 32, 128), BF16),
            pltpu.VMEM((4, NZ, 32, 128), BF16),
            pltpu.VMEM((4, NZ, 32, 128), BF16),
            pltpu.VMEM((3, 4, 32, 128), BF16),
            pltpu.VMEM((N_ORI, 1, 128), F32),
            pltpu.VMEM((N_ORI, 1, 128), F32),
            pltpu.VMEM((1, 1, 256), F32),
            pltpu.VMEM((N_ORI, 1, 256), F32),
            pltpu.VMEM((N_IMG, 1, 128), F32),
            pltpu.VMEM((N_IMG, 1, 128), F32),
            pltpu.VMEM((1, 1, 128), F32),
            pltpu.VMEM((N_ORI, 1, 128), F32),
            pltpu.VMEM((N_ORI, CAP, 128), BF16),
            pltpu.VMEM((N_ORI, CAP, 128), BF16),
            pltpu.VMEM((N_ORI, CAP, 128), BF16),
            pltpu.VMEM((N_ORI, CAP, 128), BF16),
            pltpu.VMEM((SLOTS, 128), BF16),
            pltpu.VMEM((128, SLOTS), BF16),
            pltpu.VMEM((128, SLOTS), BF16),
            pltpu.VMEM((SLOTS, 128), BF16),
            pltpu.VMEM((128, N_ORI), F32),
            pltpu.SemaphoreType.DMA((7,)),
            pltpu.SemaphoreType.DMA,
            pltpu.SemaphoreType.DMA((len(gather_plan()),)),
            pltpu.SemaphoreType.DMA((4,)),
            pltpu.SemaphoreType.DMA((4,)),
            pltpu.SemaphoreType.DMA((4,)),
            pltpu.SemaphoreType.DMA((4, 5)),
            pltpu.SemaphoreType.DMA((6,)),
            pltpu.SemaphoreType.DMA((6,)),
            pltpu.SemaphoreType.REGULAR((4, 2)),
        ],
        compiler_params=pltpu.CompilerParams(
            collective_id=0, has_side_effects=True, vmem_limit_bytes=40 * 1024 * 1024
        ),
    )(*(pltpu.with_memory_space_constraint(operand, pltpu.HBM) for operand in operands))
    volume, resampled = pl.pallas_call(
        hand_over,
        out_shape=(jax.ShapeDtypeStruct((ROWS, 128), F32), jax.ShapeDtypeStruct((128, 128), F32)),
        in_specs=[vmem],
        out_specs=(vmem, vmem),
        compiler_params=pltpu.CompilerParams(vmem_limit_bytes=4 * 1024 * 1024),
    )(both)
    return (volume, resampled.reshape(1, COEF))


def solution(mesh):
    in_specs = (
        P(("img", "ori"), None),
        P("ori", None),
        P(),
        P(("ori", "img"), None),
        P(("ori", "img")),
        P(("ori", "img"), None),
        P(("ori", "img")),
    )
    out_specs = (P(("ori", "img"), None), P(("ori", "img"), None))
    return jax.shard_map(shards, mesh=mesh, in_specs=in_specs, out_specs=out_specs, check_vma=False)
```

```python
import heapq
import math

import jax
import jax.numpy as jnp
from jax import lax
from jax.experimental import pallas as pl
from jax.experimental.pallas import tpu as pltpu
from jax.sharding import PartitionSpec as P

NX, NY, NZ = 4, 8, 8
N_ORI = NX * NY
N_IMG = 2 * NZ
COEF = 16384
QUART = COEF // 4
SHIFTS = 12
CAP = 16
SLOTS = N_ORI * CAP
ROWS = 64
MESH = pl.DeviceIdType.MESH
SCORE_COLS = 2048
HIGH = lax.Precision.HIGHEST
F32, BF16 = jnp.float32, jnp.bfloat16

SPLIT = 1536
RANGE = {"A": (0, SPLIT), "B": (SPLIT, QUART)}
PARENT = {"A": ((0, 0, 1), (0, 0, 1, 2, 2)), "B": ((0, 0, 1), (0, 0, 0, 2, 2))}


def ring_steps(parents, size, d, sign, lo, hi, mid):
    for k in range(1, size // 2 + 1):
        for way in (1, -1):
            if d != way * parents[k] % size or d and sign != way:
                continue
            a, b = lo, hi
            if k == size // 2:
                a, b = (lo, min(hi, mid)) if way > 0 else (max(lo, mid), hi)
            if a < b:
                yield way, way * k % size, k - parents[k], a, b


def forwards(block):
    route, lo, hi, dx, dy, sx, sy = block
    mid = sum(RANGE[route]) // 2
    par_x, par_y = PARENT[route]
    out = []
    if route == "A" or dx == 0:
        for way, d, hops, a, b in ring_steps(par_y, NY, dy, sy, lo, hi, mid):
            out.append(("y", way * hops, (route, a, b, dx, d, sx, way)))
    if route == "B" or dy == 0:
        for way, d, hops, a, b in ring_steps(par_x, NX, dx, sx, lo, hi, mid):
            out.append(("x", way * hops, (route, a, b, d, dy, way, sy)))
    return out


def depth(block):
    return max((1.4 + 0.7 * abs(h) + depth(k) for _, h, k in forwards(block)), default=0)


def gather_plan():
    heap = [(0.0, i, (r, *RANGE[r], 0, 0, 0, 0)) for i, r in enumerate("BA")]
    free, plan, count = {}, [], 10
    while heap:
        when, _, block = heapq.heappop(heap)
        hops = sorted(forwards(block), key=lambda f: -depth(f[2]) - 0.7 * abs(f[1]))
        plan.append((block, hops))
        for axis, dist, to in hops:
            wire = axis, dist > 0
            took = (to[2] - to[1]) * 16 / 46.5e3 + 0.03
            begin = max(when, free.get(wire, 0.0))
            free[wire] = begin + took * abs(dist)
            count += 1
            heapq.heappush(heap, (begin + took + 1.4 + 0.7 * abs(dist), count, to))
    return plan


def row(half, s, part):
    return ((half * SHIFTS + s) * 2 + part) * 16


def iota(shape, dim):
    return lax.broadcasted_iota(jnp.int32, shape, dim)


def kernel(
    images_h, refs_h, shifts_h, owners_h, rows_h, interp_h, reg_h,
    out,
    images, refs, shifts, owners, slot_rows, interp, reg,
    gat, rot, cos_t, sin_t, acc, wts, part, own_tot, pair_s, pair_r, z_s, z_r, relay_r,
    meta_s, meta_r, stat_s, stat_r, mz_s, mz_r, mb_s, mb_r, val_s, val_r, rep_s, rep_r,
    oh, oh_t, scat, scat_t, cnt,
    loc_sem, gat_send, gat_recv, pair_send, pair_recv, z_send, z_recv, sends, recvs, token,
):
    me_i, me_o = lax.axis_index("img"), lax.axis_index("ori")
    x, y = me_o // NY, lax.rem(me_o, NY)
    z, c = me_i // 2, lax.rem(me_i, 2)
    up, down = lax.rem(z + 1, NZ) * 2 + c, lax.rem(z + NZ - 1, NZ) * 2 + c

    def along(axis, dist):
        if axis == "x":
            return lax.rem(x + NX + dist, NX) * NY + y
        return x * NY + lax.rem(y + NY + dist, NY)

    plan = gather_plan()
    number = {block: i for i, (block, _) in enumerate(plan)}
    near = sorted({(axis, dist) for _, hops in plan for axis, dist, _ in hops})
    barrier = pltpu.get_barrier_semaphore()
    for axis, dist in near:
        pl.semaphore_signal(barrier, 1, device_id={"ori": along(axis, dist)}, device_id_type=MESH)
    for to in (up, down, z * 2 + 1 - c):
        pl.semaphore_signal(barrier, 1, device_id={"img": to}, device_id_type=MESH)

    loads = [
        pltpu.make_async_copy(src, dst, loc_sem.at[i])
        for i, (src, dst) in enumerate(
            [(images_h, images), (shifts_h, shifts), (refs_h, refs), (owners_h, owners), (rows_h, slot_rows),
             (interp_h, interp), (reg_h, reg)]
        )
    ]
    for copy in loads:
        copy.start()

    loads[0].wait()
    gat[me_o] = jnp.concatenate(
        [images[:, q * QUART : (q + 1) * QUART].astype(F32) for q in range(4)], axis=0
    ).astype(BF16)
    loads[1].wait()

    unit = 2.0 * math.pi / 128.0
    eye12 = iota((SHIFTS, SHIFTS), 0) == iota((SHIFTS, SHIFTS), 1)
    step_x = unit * jnp.sum(jnp.where(eye12, shifts[0:1, :], 0.0), axis=1, keepdims=True)
    step_y = unit * jnp.sum(jnp.where(eye12, shifts[1:2, :], 0.0), axis=1, keepdims=True)

    def tables(step):
        lane12 = iota((SHIFTS, 128), 1)
        base = step_x * (lane12 % 64).astype(F32) + step_y * (lane12 // 64).astype(F32)
        tile = step_y * (2 * lane12 - 64).astype(F32)
        base_c, base_s, tile_c, tile_s = jnp.cos(base), jnp.sin(base), jnp.cos(tile), jnp.sin(tile)
        for t in range(64):
            half, col = t // 32, (t % 32) * 128
            tc, ts = tile_c[:, t : t + 1], tile_s[:, t : t + 1]
            cos_t[half, :, col : col + 128] = base_c * tc - base_s * ts
            sin_t[half, :, col : col + 128] = base_s * tc + base_c * ts

    def rotate(step):
        if step == 0:
            loads[2].wait()
        col = step * 256
        for half in range(2):
            real = refs[:, half * QUART + col : half * QUART + col + 256].astype(F32)
            imag = refs[:, (2 + half) * QUART + col : (2 + half) * QUART + col + 256].astype(F32)
            for s in range(SHIFTS):
                cs, sn = cos_t[half, s : s + 1, col : col + 256], sin_t[half, s : s + 1, col : col + 256]
                r = row(half, s, 0)
                rot[r : r + 16, col : col + 256] = (real * cs - imag * sn).astype(BF16)
                rot[r + 16 : r + 32, col : col + 256] = (real * sn + imag * cs).astype(BF16)

    def routing(step):
        loads[3].wait()
        loads[4].wait()
        eye = iota((128, 128), 0) == iota((128, 128), 1)
        row_col = jnp.sum(jnp.where(eye, slot_rows[...].astype(F32), 0.0), axis=1, keepdims=True)
        own_col = jnp.sum(jnp.where(eye, owners[...].astype(F32), 0.0), axis=1, keepdims=True)
        blocks = [(q * 32 + u * 8) for u in range(4) for q in range(4)]
        row_col = jnp.concatenate([row_col[b : b + 8] for b in blocks], axis=0)
        own_col = jnp.concatenate([own_col[b : b + 8] for b in blocks], axis=0)
        lane128 = iota((128, 128), 1).astype(F32)
        owner_hot = (own_col == lane128).astype(F32)
        before = (iota((128, 128), 1) < iota((128, 128), 0)).astype(BF16)
        counts = jnp.dot(before, owner_hot.astype(BF16), preferred_element_type=F32)
        rank_col = jnp.sum(counts * owner_hot, axis=1, keepdims=True)
        slot_col = own_col * CAP + rank_col
        slot_row = jnp.sum(jnp.where(eye, slot_col, 0.0), axis=0, keepdims=True)
        oh[...] = (slot_row == iota((SLOTS, 128), 0).astype(F32)).astype(BF16)
        oh_t[...] = (slot_col == iota((128, SLOTS), 1).astype(F32)).astype(BF16)
        rank_rows = jnp.where(rank_col == lane128, row_col + 1.0, 0.0).astype(BF16)
        table = lax.dot_general(
            owner_hot.astype(BF16), rank_rows, (((0,), (0,)), ((), ())), preferred_element_type=F32
        ) - 1.0
        for d in range(N_ORI):
            meta_s[d] = table[d : d + 1, :]

    def pass_token(step):
        if step:
            for way in range(2):
                pl.semaphore_wait(token.at[step - 1, way], 1)
        if step < 4:
            for way, to in enumerate((up, down)):
                pl.semaphore_signal(token.at[step, way], 1, device_id={"img": to}, device_id_type=MESH)

    pl.semaphore_wait(barrier, len(near) + 3)

    def gather_copy(block, dx, dy, to):
        src = lax.rem(x + NX - dx, NX) * NY + lax.rem(y + NY - dy, NY)
        ref = gat.at[src, :, pl.ds(block[1], block[2] - block[1])]
        return pltpu.make_async_remote_copy(
            src_ref=ref, dst_ref=ref, send_sem=gat_send, recv_sem=gat_recv.at[number[block]],
            device_id={"ori": to}, device_id_type=MESH,
        )

    xs = [lax.rem(x + d, NX) * NY for d in range(NX)]
    ys = [lax.rem(y + d, NY) for d in range(NY)]
    others = sorted(
        ((a, b) for a in range(NX) for b in range(NY) if a or b), key=lambda p: -min(p[0], NX - p[0]) - min(p[1], NY - p[1])
    )

    def spread(send_ref, recv_ref, which):
        for a, b in others:
            to = xs[a] + ys[b]
            src = send_ref.at[0] if send_ref.shape[0] == 1 else send_ref.at[to]
            pltpu.make_async_remote_copy(
                src_ref=src, dst_ref=recv_ref.at[me_o], send_sem=sends.at[which], recv_sem=recvs.at[which],
                device_id={"ori": to}, device_id_type=MESH,
            ).start()

    def await_bytes(ref, sem):
        pltpu.make_async_copy(ref, ref, sem).wait()

    jobs = [(pass_token, 0), (tables, 0)]
    jobs += [(rotate, i) for i in range(QUART // 256)]
    jobs[6:6] = [(pass_token, 1)]
    jobs[10:10] = [(pass_token, 2)]
    jobs[14:14] = [(pass_token, 3)]
    jobs += [(pass_token, 4), (routing, 0)]
    due = [1] * 8 + [5 + i * (len(plan) - 12) // (len(jobs) - 8) for i in range(len(jobs) - 8)]
    for i, (block, hops) in enumerate(plan):
        dx, dy = block[3:5]
        if dx or dy:
            gather_copy(block, dx, dy, me_o).wait_recv()
        for axis, dist, to in hops:
            gather_copy(to, dx, dy, along(axis, dist)).start()
        while due and due[0] <= i:
            due.pop(0)
            job, step = jobs.pop(0)
            job(step)
    for job, step in jobs:
        job(step)
    for h in range(2):
        acc[h * 384 : h * 384 + 384, :] = lax.dot_general(
            rot[h * 384 : h * 384 + 384, :], gat[...].reshape(N_ORI * 8, QUART), (((1,), (1,)), ((), ())),
            preferred_element_type=F32)

    quarter = iota((16, 256), 1) % 8 // 2
    places = [(half, im) for half in range(2) for im in range(2)]
    mine = []
    for s in range(SHIFTS):
        mine.append(
            sum(
                jnp.where(quarter == 2 * im + half, acc[row(half, s, im) : row(half, s, im) + 16, :], 0.0)
                for half, im in places
            )
        )
    mine = jnp.concatenate(mine, axis=0)
    left, right = iota((256, 256), 0), iota((256, 256), 1)
    fold = ((left // 8 == right // 8) & (left % 2 == right % 2)).astype(F32)
    scores = jnp.dot(mine, fold, precision=HIGH, preferred_element_type=F32) * (2.0 / math.sqrt(COEF))
    peak = jnp.max(scores, axis=0, keepdims=True)
    expo = jnp.exp(scores - peak)
    total = jnp.sum(expo, axis=0, keepdims=True)
    stat = jnp.where(iota((1, 256), 1) // 2 % 2 == 0, peak, total)
    stat_s[0] = stat
    spread(stat_s, stat_r, 1)
    stat_r[me_o] = stat
    spread(meta_s, meta_r, 0)
    meta_r[me_o] = meta_s[me_o]
    loads[5].wait()
    loads[6].wait()

    await_bytes(stat_r.at[pl.ds(0, N_ORI - 1)], recvs.at[1])
    stats = stat_r[...].reshape(N_ORI, 256)
    even = iota((N_ORI, 256), 1) // 2 % 2 == 0
    peaks = jnp.where(even, stats, pltpu.roll(stats, 2, 1))
    totals = jnp.where(even, pltpu.roll(stats, 254, 1), stats)
    top = jnp.max(peaks, axis=0, keepdims=True)
    whole = jnp.sum(totals * jnp.exp(peaks - top), axis=0, keepdims=True)
    weights = expo * (jnp.exp(peak - top) / whole)
    for s in range(SHIFTS):
        for half, im in places:
            r = row(half, s, im)
            wts[r : r + 16, :] = jnp.where(quarter == 2 * im + half, weights[s * 16 : s * 16 + 16], 0.0).astype(BF16)

    def pair_copy(u):
        return pltpu.make_async_remote_copy(
            src_ref=pair_s.at[u], dst_ref=pair_r.at[u], send_sem=pair_send.at[u], recv_sem=pair_recv.at[u],
            device_id={"img": z * 2 + 1 - c}, device_id_type=MESH,
        )

    def project(u):
        for half in range(2):
            res, ims = [], []
            for v in range(1024 // 512):
                cols = slice(u * 1024 + v * 512, u * 1024 + v * 512 + 512)
                block = gat[:, :, cols].reshape(N_ORI * 8, 512)
                prod = jnp.dot(wts[half * 384 : half * 384 + 384, :], block, preferred_element_type=F32)
                re = jnp.zeros((16, 512), F32)
                im = jnp.zeros((16, 512), F32)
                for s in range(SHIFTS):
                    cs, sn = cos_t[half, s : s + 1, cols], sin_t[half, s : s + 1, cols]
                    sr = prod[s * 32 : s * 32 + 16, :]
                    si = prod[s * 32 + 16 : s * 32 + 32, :]
                    re = re + sr * cs + si * sn
                    im = im - sr * sn + si * cs
                res.append(re)
                ims.append(im)
            for first, sums in ((half * 8, res), (16 + half * 8, ims)):
                part[u, :, first : first + 8, :] = jnp.concatenate(sums, axis=1).reshape(16, 8, 128)
        for k in range(NZ):
            pair_s[u, k] = part[u, 2 * k + 1 - c].astype(BF16)
        pair_copy(u).start()

    zs = [lax.rem(z + d, NZ) for d in range(NZ)]

    def chip_sum(u, to):
        return part[u, 2 * to + c] + pair_r[u, to].astype(F32)

    def z_copy(u, src, dst, dist, sem):
        return pltpu.make_async_remote_copy(
            src_ref=src, dst_ref=dst, send_sem=z_send.at[u], recv_sem=sem,
            device_id={"img": zs[dist % NZ] * 2 + c}, device_id_type=MESH,
        )

    def first_leg(u):
        pair_copy(u).wait_recv()
        own_tot[u] = chip_sum(u, z)
        if u == 3:
            for d in (4, 3, 5, 2, 6, 1, 7):
                z_s[u, d] = chip_sum(u, zs[d]).astype(BF16)
                z_copy(u, z_s.at[u, d], z_r.at[u, NZ - d], d, z_recv.at[u, 0]).start()
            return
        z_s[u, 4] = chip_sum(u, zs[4]).astype(BF16)
        for way, (far, via, near_by) in enumerate(((3, 1, 1), (5, 7, 7))):
            z_s[u, far] = chip_sum(u, zs[far]).astype(BF16)
            half = pl.ds(way * 16, 16)
            z_copy(u, z_s.at[u, 4, half], relay_r.at[u, 2 + way, half], 2 * via, z_recv.at[u, 3 + way]).start()
            z_copy(u, z_s.at[u, far], relay_r.at[u, way], via, z_recv.at[u, 1 + way]).start()
            z_s[u, near_by] = chip_sum(u, zs[near_by]).astype(BF16)
        for near_by in (1, 7):
            z_copy(u, z_s.at[u, near_by], z_r.at[u, NZ - near_by], near_by, z_recv.at[u, 0]).start()

    def second_leg(u):
        for way, (to, other) in enumerate(((2, 16), (6, 0))):
            await_bytes(relay_r.at[u, way], z_recv.at[u, 1 + way])
            half = pl.ds(way * 16, 16)
            await_bytes(relay_r.at[u, 2 + way, half], z_recv.at[u, 3 + way])
            total = chip_sum(u, zs[to]) + relay_r[u, way].astype(F32)
            far = relay_r[u, 2 + way, way * 16 : way * 16 + 16, :].astype(F32)
            zero = jnp.zeros((16, 128), F32)
            total = total + jnp.concatenate([zero, far] if way else [far, zero], axis=0)
            z_s[u, to] = total.astype(BF16)
            z_copy(u, z_s.at[u, to], z_r.at[u, NZ - to], to, z_recv.at[u, 0]).start()

    project(0)
    project(1)
    project(2)
    first_leg(0)
    project(3)
    first_leg(1)
    first_leg(2)

    mass16 = weights[0:16]
    for s in range(1, SHIFTS):
        mass16 = mass16 + weights[s * 16 : s * 16 + 16]
    mass16 = jnp.sum(jnp.where(quarter == 0, mass16, 0.0), axis=1, keepdims=True)
    mass16 = jnp.broadcast_to(mass16, (16, 128))
    for o in range(N_IMG):
        mz_s[o] = mass16[o : o + 1, :]

    def send_mass(p, carry):
        to = lax.rem(me_i + p, N_IMG)
        pltpu.make_async_remote_copy(
            src_ref=mz_s.at[to], dst_ref=mz_r.at[me_i], send_sem=sends.at[2], recv_sem=recvs.at[2],
            device_id={"img": to}, device_id_type=MESH,
        ).start()
        return carry

    lax.fori_loop(1, N_IMG, send_mass, 0)
    mz_r[me_i] = mz_s[me_i]

    await_bytes(meta_r.at[pl.ds(0, N_ORI - 1)], recvs.at[0])
    rep = (iota((SLOTS, N_ORI), 0) // CAP == iota((SLOTS, N_ORI), 1)).astype(BF16)
    rid = jnp.dot(rep, meta_r[...].reshape(N_ORI, 128).astype(BF16), preferred_element_type=F32)
    rid = jnp.where(iota((SLOTS, 128), 0) % CAP == iota((SLOTS, 128), 1), rid, 0.0)
    hot = (jnp.sum(rid, axis=1, keepdims=True) == iota((SLOTS, 128), 1).astype(F32)).astype(F32)
    scat_t[...] = hot.astype(BF16)
    scat[...] = jnp.transpose(hot).astype(BF16)
    cnt[...] = jnp.dot(scat[...], rep, preferred_element_type=F32)
    reg_col = jnp.sum(
        jnp.where(iota((ROWS, ROWS), 0) == iota((ROWS, ROWS), 1), reg[...], 0.0), axis=1, keepdims=True
    )

    gram = lax.dot_general(
        interp[...], interp[...], (((1,), (1,)), ((), ())), precision=HIGH, preferred_element_type=F32
    )

    first_leg(3)
    for u in range(3):
        second_leg(u)

    await_bytes(mz_r.at[pl.ds(0, N_IMG - 1)], recvs.at[2])
    mass_all = jnp.sum(mz_r[...].reshape(N_IMG, 128), axis=0, keepdims=True)
    mb_s[0] = mass_all
    spread(mb_s, mb_r, 3)
    mb_r[me_o] = mass_all

    sums = []
    for u in range(4):
        sources = (1, 2, 6, 7) if u < 3 else range(1, NZ)
        await_bytes(z_r.at[u, pl.ds(0, len(sources))], z_recv.at[u, 0])
        tot = own_tot[u]
        for d in sources:
            tot = tot + z_r[u, d].astype(F32)
        sums.append(tot)
    segments = jnp.concatenate(sums, axis=0).astype(BF16)

    val_s[...] = jnp.dot(oh[...], segments, preferred_element_type=F32).astype(BF16).reshape(N_ORI, CAP, 128)
    spread(val_s, val_r, 4)
    val_r[me_o] = val_s[me_o]

    await_bytes(mb_r.at[pl.ds(0, N_ORI - 1)], recvs.at[3])
    weight_sum = jnp.dot(
        cnt[0:ROWS, :], mb_r[...].reshape(N_ORI, 128), precision=HIGH, preferred_element_type=F32
    )
    inverse = 1.0 / (weight_sum + reg_col)

    await_bytes(val_r.at[pl.ds(0, N_ORI - 1)], recvs.at[4])
    inserted = jnp.dot(scat[0:ROWS, :], val_r[...].reshape(SLOTS, 128), preferred_element_type=F32)
    back = jnp.dot(inserted, gram, precision=HIGH, preferred_element_type=F32) * inverse
    reply = jnp.dot(scat_t[:, 0:ROWS], back.astype(BF16), preferred_element_type=F32)
    rep_s[...] = reply.astype(BF16).reshape(N_ORI, CAP, 128)
    spread(rep_s, rep_r, 5)
    rep_r[me_o] = rep_s[me_o]
    out[0:ROWS, :] = jnp.dot(inserted, interp[...], precision=HIGH, preferred_element_type=F32) * inverse

    await_bytes(gat.at[pl.ds(0, N_ORI - 1)], gat_send)
    for u in range(4):
        pair_copy(u).wait_send()
        await_bytes(z_s.at[u, pl.ds(0, NZ - 1)], z_send.at[u])
    await_bytes(meta_s.at[pl.ds(0, N_ORI - 1)], sends.at[0])
    await_bytes(stat_r.at[pl.ds(0, N_ORI - 1)], sends.at[1])
    await_bytes(mz_s.at[pl.ds(0, N_IMG - 1)], sends.at[2])
    await_bytes(mb_r.at[pl.ds(0, N_ORI - 1)], sends.at[3])
    await_bytes(val_s.at[pl.ds(0, N_ORI - 1)], sends.at[4])

    await_bytes(rep_r.at[pl.ds(0, N_ORI - 1)], recvs.at[5])
    picked = jnp.dot(oh_t[...], rep_r[...].reshape(SLOTS, 128), preferred_element_type=F32)
    for u in range(4):
        for q in range(4):
            to = ROWS + q * 32 + u * 8
            out[to : to + 8, :] = picked[u * 32 + q * 8 : u * 32 + q * 8 + 8, :]
    await_bytes(rep_s.at[pl.ds(0, N_ORI - 1)], sends.at[5])


def hand_over(both, vol, res):
    vol[...] = both[0:ROWS, :]
    res[...] = both[ROWS : ROWS + 128, :]


def shards(images, references, shifts, owners, slot_rows, interpolation, regularizer):
    vmem = pl.BlockSpec(memory_space=pltpu.VMEM)
    anywhere = pl.BlockSpec(memory_space=pl.ANY)
    operands = (
        images,
        references,
        shifts.T,
        owners.reshape(1, 128),
        slot_rows.reshape(1, 128),
        interpolation,
        regularizer.reshape(1, ROWS),
    )
    both = pl.pallas_call(
        kernel,
        out_shape=jax.ShapeDtypeStruct((ROWS + 128, 128), F32),
        in_specs=[anywhere] * 7,
        out_specs=vmem,
        scratch_shapes=[
            pltpu.VMEM((2, COEF), BF16),
            pltpu.VMEM((16, COEF), BF16),
            pltpu.VMEM((2, SHIFTS), F32),
            pltpu.VMEM((1, 128), jnp.int32),
            pltpu.VMEM((1, 128), jnp.int32),
            pltpu.VMEM((128, 128), F32),
            pltpu.VMEM((1, ROWS), F32),
            pltpu.VMEM((N_ORI, 8, QUART), BF16),
            pltpu.VMEM((768, QUART), BF16),
            pltpu.VMEM((2, SHIFTS, QUART), F32),
            pltpu.VMEM((2, SHIFTS, QUART), F32),
            pltpu.VMEM((768, 256), F32),
            pltpu.VMEM((768, 256), BF16),
            pltpu.VMEM((4, N_IMG, 32, 128), F32),
            pltpu.VMEM((4, 32, 128), F32),
            pltpu.VMEM((4, NZ, 32, 128), BF16),
            pltpu.VMEM((4, NZ, 32, 128), BF16),
            pltpu.VMEM((4, NZ, 32, 128), BF16),
            pltpu.VMEM((4, NZ, 32, 128), BF16),
            pltpu.VMEM((3, 4, 32, 128), BF16),
            pltpu.VMEM((N_ORI, 1, 128), F32),
            pltpu.VMEM((N_ORI, 1, 128), F32),
            pltpu.VMEM((1, 1, 256), F32),
            pltpu.VMEM((N_ORI, 1, 256), F32),
            pltpu.VMEM((N_IMG, 1, 128), F32),
            pltpu.VMEM((N_IMG, 1, 128), F32),
            pltpu.VMEM((1, 1, 128), F32),
            pltpu.VMEM((N_ORI, 1, 128), F32),
            pltpu.VMEM((N_ORI, CAP, 128), BF16),
            pltpu.VMEM((N_ORI, CAP, 128), BF16),
            pltpu.VMEM((N_ORI, CAP, 128), BF16),
            pltpu.VMEM((N_ORI, CAP, 128), BF16),
            pltpu.VMEM((SLOTS, 128), BF16),
            pltpu.VMEM((128, SLOTS), BF16),
            pltpu.VMEM((128, SLOTS), BF16),
            pltpu.VMEM((SLOTS, 128), BF16),
            pltpu.VMEM((128, N_ORI), F32),
            pltpu.SemaphoreType.DMA((7,)),
            pltpu.SemaphoreType.DMA,
            pltpu.SemaphoreType.DMA((len(gather_plan()),)),
            pltpu.SemaphoreType.DMA((4,)),
            pltpu.SemaphoreType.DMA((4,)),
            pltpu.SemaphoreType.DMA((4,)),
            pltpu.SemaphoreType.DMA((4, 5)),
            pltpu.SemaphoreType.DMA((6,)),
            pltpu.SemaphoreType.DMA((6,)),
            pltpu.SemaphoreType.REGULAR((4, 2)),
        ],
        compiler_params=pltpu.CompilerParams(
            collective_id=0, has_side_effects=True, vmem_limit_bytes=40 * 1024 * 1024
        ),
    )(*(pltpu.with_memory_space_constraint(operand, pltpu.HBM) for operand in operands))
    volume, resampled = pl.pallas_call(
        hand_over,
        out_shape=(jax.ShapeDtypeStruct((ROWS, 128), F32), jax.ShapeDtypeStruct((128, 128), F32)),
        in_specs=[vmem],
        out_specs=(vmem, vmem),
        compiler_params=pltpu.CompilerParams(vmem_limit_bytes=4 * 1024 * 1024),
    )(both)
    return (volume, resampled.reshape(1, COEF))


def solution(mesh):
    in_specs = (
        P(("img", "ori"), None),
        P("ori", None),
        P(),
        P(("ori", "img"), None),
        P(("ori", "img")),
        P(("ori", "img"), None),
        P(("ori", "img")),
    )
    out_specs = (P(("ori", "img"), None), P(("ori", "img"), None))
    return jax.shard_map(shards, mesh=mesh, in_specs=in_specs, out_specs=out_specs, check_vma=False)
```
